256 devices in a mesh: tm: 64 (over x, z, core), dp: 4 (over y).
Axes of the slice: x: 4, y: 4, z: 8, core: 2. Of those that a mesh axis runs over, the one named last changes fastest.
Arguments:
- inputs: bfloat16 [4, 32768, 256], P('dp', 'tm'), may hold values from -6 to 6
- grad_stream_out: bfloat16 [4, 32768, 256], P('dp', 'tm'), may hold values from -6 to 6
- grad_skip_out: bfloat16 [4, 32768, 256], P('dp', 'tm'), may hold values from -6 to 6
- sample_weight: float32 [4, 32768], P('dp', 'tm'), may hold values from 0.5 to 6, as said below
- conv_weight: bfloat16 [6, 512, 512], replicated, may hold values from -0.25 to 0.25
- out_weight: bfloat16 [6, 256, 512], replicated, may hold values from -0.375 to 0.375
Outputs:
- grad_inputs: float32 [4, 32768, 256], P('dp', 'tm')
- grad_conv: float32 [6, 512, 512], P(None, 'tm', 'dp')
- grad_out: float32 [6, 256, 512], P(None, 'tm', 'dp')
The draws below stay inside these ranges and needn't reach their ends.
Inputs may be any that keep to these rules, and one draw needn't show every extreme that they name: `sample_weight`: positive loss weights of each sample.
All inputs are finite; a program needn't handle non-finite values.
Results may differ from the reference program's by a relative error of at most 0.02.
Values may be sent and summed in bfloat16 or wider, within the bound.
A program may use at most 128 MiB of HBM per device.

```python
import jax
import jax.numpy as jnp

C = 256
LAYERS = 6
SAMPLES = 32768
BATCH = 4


def draw_sample_weight(key, part):
    rising = 1.0 + 2.0 * jnp.arange(SAMPLES, dtype=jnp.float32) / (SAMPLES - 1)
    factor = jnp.exp(jax.random.uniform(key, (BATCH, SAMPLES), jnp.float32, -0.69, 0.69))
    return rising[None, :] * factor


def block_levels(stream_key, extent, split, smallest, top_value):
    level, own = 1.0, jax.random.fold_in(stream_key, 6)
    for dim, parts in split:
        draws = jnp.exp(jax.random.uniform(jax.random.fold_in(own, dim), (parts,), jnp.float32, smallest / len(split), top_value / len(split)))
        level = level * jnp.repeat(draws, extent[dim] // parts).reshape([-1 if axis == dim else 1 for axis in range(len(extent))])
    return level


def normal_values(key, shape, spread, most, pieces=(), kind=jnp.bfloat16):
    factor_of = block_levels(key, shape, pieces, -0.22, 0.18) if pieces else 1.0
    values = jax.random.normal(key, shape, jnp.float32) * spread * factor_of
    return jnp.minimum(jnp.maximum(values, -most), most).astype(kind)


def setup_inputs(seed: int = 0) -> dict:
    arg_keys = jax.random.split(jax.random.key(seed), 7)
    return {
        "inputs": normal_values(arg_keys[0], (BATCH, SAMPLES, C), 1.0, 6.0, ((0, 4), (1, 64))),
        "grad_stream_out": normal_values(arg_keys[1], (BATCH, SAMPLES, C), 1.0, 6.0, ((0, 4), (1, 64))),
        "grad_skip_out": normal_values(arg_keys[2], (BATCH, SAMPLES, C), 1.0, 6.0, ((0, 4), (1, 64))),
        "sample_weight": draw_sample_weight(jax.random.fold_in(arg_keys[6], 71), 0),
        "conv_weight": normal_values(arg_keys[4], (LAYERS, 2 * C, 2 * C), (2 * C) ** -0.5, 0.25),
        "out_weight": normal_values(arg_keys[5], (LAYERS, C, 2 * C), C ** -0.5, 0.375),
    }


def flat_dot(operand, matrix):
    lead = operand.shape[:-1]
    result = jnp.dot(operand.reshape(-1, operand.shape[-1]), matrix, preferred_element_type=jnp.float32)
    return result.reshape(lead + (matrix.shape[-1],))


def outer_sum(left_op, right_op):
    return jnp.dot(left_op.reshape(-1, left_op.shape[-1]).T, right_op.reshape(-1, right_op.shape[-1]), preferred_element_type=jnp.float32)


def shift_past(values, dilation):
    return jnp.pad(values, ((0, 0), (dilation, 0), (0, 0)))[:, :values.shape[1]]


def shift_later(values, dilation):
    return jnp.pad(values, ((0, 0), (0, dilation), (0, 0)))[:, dilation:]


def forward_layer(present, earlier, conv_layer, out_layer, channels):
    preact = flat_dot(present, conv_layer[:channels]) + flat_dot(earlier, conv_layer[channels:])
    gated = (jnp.tanh(preact[..., :channels]) * jax.nn.sigmoid(preact[..., channels:])).astype(jnp.bfloat16)
    return preact, gated


def reference(inputs, grad_stream_out, grad_skip_out, sample_weight, conv_weight, out_weight):
    channels = inputs.shape[2]
    samples_all = sample_weight.shape[0] * sample_weight.shape[1]
    weighting = sample_weight * (samples_all / jnp.sum(sample_weight))
    stream = inputs.astype(jnp.float32)
    stored = []
    for layer_index in range(LAYERS):
        dilation = 2 ** layer_index
        present = stream.astype(jnp.bfloat16)
        earlier = shift_past(present, dilation)
        preact, gated = forward_layer(present, earlier, conv_weight[layer_index], out_weight[layer_index], channels)
        projected = flat_dot(gated, out_weight[layer_index])
        stream = stream + projected[..., :channels]
        stored.append(present)
    grad_stream = grad_stream_out.astype(jnp.float32) * weighting[..., None]
    grad_skips = grad_skip_out.astype(jnp.float32) * weighting[..., None]
    conv_grads = [None] * LAYERS
    out_grads = [None] * LAYERS
    for layer_index in reversed(range(LAYERS)):
        dilation = 2 ** layer_index
        present = stored[layer_index]
        earlier = shift_past(present, dilation)
        preact, gated = forward_layer(present, earlier, conv_weight[layer_index], out_weight[layer_index], channels)
        grad_proj = jnp.concatenate([grad_stream, grad_skips], axis=-1).astype(jnp.bfloat16)
        out_grads[layer_index] = outer_sum(gated, grad_proj)
        grad_gated = flat_dot(grad_proj, out_weight[layer_index].T)
        filtered = jnp.tanh(preact[..., :channels])
        opening = jax.nn.sigmoid(preact[..., channels:])
        grad_preact = jnp.concatenate([grad_gated * opening * (1.0 - filtered * filtered), grad_gated * filtered * opening * (1.0 - opening)], axis=-1).astype(jnp.bfloat16)
        conv_grads[layer_index] = jnp.concatenate([outer_sum(present, grad_preact), outer_sum(earlier, grad_preact)], axis=0)
        later_rows = shift_later(grad_preact, dilation)
        grad_stream = grad_stream + flat_dot(grad_preact, conv_weight[layer_index, :channels].T) + flat_dot(later_rows, conv_weight[layer_index, channels:].T)
    return grad_stream, jnp.stack(conv_grads), jnp.stack(out_grads)
```

```python
import functools

import jax
import jax.numpy as jnp
from jax import lax
from jax.experimental import pallas as pl
from jax.experimental.pallas import tpu as pltpu
from jax.sharding import PartitionSpec as P

MESH = pl.DeviceIdType.MESH
F32, BF16 = jnp.float32, jnp.bfloat16
C, LAYERS, T, HALO = 256, 6, 512, 64
EXT = T + 2 * HALO
POST = T + HALO
SIZES = {"x": 4, "y": 4, "z": 8}
BACK_ROWS = (544, 544, 544, 544, 544, 576)
PARTS = 9
ORDERS = ("yxz", "xyz", "zyx", "yxz", "xyz", "zyx", "yxz", "yxz", "xyz")

SCHEDULE = {
    5: (),
    4: (),
    3: ((0, 0),),
    2: ((1, 0), (2, 0)),
    1: ((3, 0), (0, 1), (1, 1), (2, 1)),
    0: (
        (4, 0), (5, 0), (6, 0), (3, 1), (0, 2), (1, 2), (2, 2), (4, 1), (5, 1), (7, 0), (8, 0), (6, 1), (3, 2),
        (4, 2), (5, 2), (7, 1), (8, 1), (6, 2), (7, 2), (8, 2),
    ),
}


def contract_rows(left, right):
    return lax.dot_general(left, right, (((0,), (0,)), ((), ())), preferred_element_type=F32)


def contract_columns(left, right):
    return lax.dot_general(left, right, (((1,), (1,)), ((), ())), preferred_element_type=F32)


def place():
    tm, y = lax.axis_index("tm"), lax.axis_index("dp")
    return {"x": tm // 16, "y": y, "z": (tm // 2) % 8, "core": tm % 2}


def device(at):
    return ((at["x"] * 8 + at["z"]) * 2 + at["core"], at["y"])


def peer(at, axis, step):
    if axis == "core":
        return dict(at, core=1 - at["core"])
    return dict(at, **{axis: (at[axis] + step) % SIZES[axis]})


def remote(src, dst, send, recv, target):
    copy = pltpu.make_async_remote_copy(
        src_ref=src, dst_ref=dst, send_sem=send, recv_sem=recv,
        device_id=target, device_id_type=MESH,
    )
    copy.start()
    return copy


def kernel(
    x_hbm, gso_hbm, gsk_hbm, sw_hbm, conv_hbm, outw_hbm,
    gin_ref, gconv_ref, gout_ref,
    xe, gse, gke, swe, conv, outw,
    stream, pres_s, gated_s, filt_s, open_s,
    gs, gproj, gp, gpb, later_b, mg, og,
    csend, crecv, hsum, wtile, wrecv,
    load_sem, halo_send, halo_recv, w_send, w_recv, p_send, p_recv, *rest,
):
    landings, sums = rest[:3 * PARTS], rest[3 * PARTS:]
    at = place()
    tm = lax.axis_index("tm")
    me = device(at)
    nxt = ((tm + 1) % 64, at["y"])
    prv = ((tm + 63) % 64, at["y"])

    barrier = pltpu.get_barrier_semaphore()
    greet = [nxt, prv, device(peer(at, "core", 1))]
    for axis in "yxz":
        greet += [device(peer(at, axis, k)) for k in range(1, SIZES[axis])]
    for target in greet:
        pl.semaphore_signal(barrier, inc=1, device_id=target, device_id_type=MESH)

    loads = [
        pltpu.make_async_copy(x_hbm.at[0], xe.at[pl.ds(HALO, T)], load_sem.at[0]),
        pltpu.make_async_copy(sw_hbm, swe.at[:, pl.ds(0, T)], load_sem.at[1]),
    ]
    for l in range(LAYERS):
        loads.append(pltpu.make_async_copy(conv_hbm.at[l], conv.at[l], load_sem.at[4 + l]))
        loads.append(pltpu.make_async_copy(outw_hbm.at[l], outw.at[l], load_sem.at[10 + l]))
    loads.append(pltpu.make_async_copy(gso_hbm.at[0], gse.at[pl.ds(0, T)], load_sem.at[2]))
    loads.append(pltpu.make_async_copy(gsk_hbm.at[0], gke.at[pl.ds(0, T)], load_sem.at[3]))
    for copy in loads:
        copy.start()
    pl.semaphore_wait(barrier, len(greet))

    halo = [
        remote(x_hbm.at[0, pl.ds(T - HALO, HALO)], xe.at[pl.ds(0, HALO)], halo_send.at[0], halo_recv.at[0], nxt),
        remote(x_hbm.at[0, pl.ds(0, HALO)], xe.at[pl.ds(HALO + T, HALO)], halo_send.at[1], halo_recv.at[1], prv),
        remote(gso_hbm.at[0, pl.ds(0, HALO)], gse.at[pl.ds(T, HALO)], halo_send.at[2], halo_recv.at[2], prv),
        remote(gsk_hbm.at[0, pl.ds(0, HALO)], gke.at[pl.ds(T, HALO)], halo_send.at[3], halo_recv.at[3], prv),
        remote(sw_hbm.at[:, pl.ds(0, 128)], swe.at[:, pl.ds(T, 128)], halo_send.at[4], halo_recv.at[4], prv),
    ]
    loads[0].wait()
    loads[1].wait()

    wtile[0] = jnp.broadcast_to(
        swe[:, 0:128] + swe[:, 128:256] + swe[:, 256:384] + swe[:, 384:512], (8, 128)
    )
    wcopies = []

    def weight_send(step, axis, base):
        count = 2 if axis == "core" else SIZES[axis]
        group = []
        for k in range(1, count):
            group.append(remote(
                wtile.at[step], wrecv.at[base + k - 1], w_send.at[base + k - 1], w_recv.at[base + k - 1],
                device(peer(at, axis, k)),
            ))
        wcopies.append((group, step, base))

    def weight_sum():
        group, step, base = wcopies[-1]
        total = wtile[step]
        for k, copy in enumerate(group):
            copy.wait_recv()
            total = total + wrecv[base + k]
        wtile[step + 1] = total

    weight_send(0, "core", 0)
    weight_steps = {0: ("y", 1), 1: ("x", 4), 3: ("z", 7)}

    stream[0:32] = jnp.zeros((32, C), F32)
    halo[0].wait_recv()
    halo[1].wait_recv()
    stream[32:32 + EXT] = xe[...].astype(F32)

    @pl.when(tm == 0)
    def _():
        stream[32:32 + HALO] = jnp.zeros((HALO, C), F32)

    step_rows = EXT // 2
    for l in range(LAYERS):
        d = 2**l
        loads[2 + 2 * l].wait()
        loads[3 + 2 * l].wait()
        for r0 in (step_rows, 0):
            present = stream[32 + r0:32 + r0 + step_rows].astype(BF16)
            earlier = stream[32 + r0 - d:32 + r0 - d + step_rows].astype(BF16)
            preact = jnp.dot(present, conv[l, 0:C], preferred_element_type=F32) + jnp.dot(
                earlier, conv[l, C:2 * C], preferred_element_type=F32
            )
            filtered = jnp.tanh(preact[:, :C])
            opening = 0.5 * jnp.tanh(0.5 * preact[:, C:]) + 0.5
            gated = (filtered * opening).astype(BF16)
            lo, hi = max(r0, HALO), r0 + step_rows
            filt_s[l, lo - HALO:hi - HALO] = filtered[lo - r0:]
            open_s[l, lo - HALO:hi - HALO] = opening[lo - r0:]
            own_hi = min(hi, HALO + T)
            pres_s[l, lo - HALO:own_hi - HALO] = present[lo - r0:own_hi - r0]
            gated_s[l, lo - HALO:own_hi - HALO] = gated[lo - r0:own_hi - r0]
            if l < LAYERS - 1:
                stream[32 + r0:32 + r0 + step_rows] += jnp.dot(
                    gated, outw[l, :, 0:C], preferred_element_type=F32
                )
        if l in weight_steps:
            weight_sum()
            weight_send(len(wcopies), *weight_steps[l])
    weight_sum()

    total = jnp.sum(wtile[4][0:1], axis=1, keepdims=True)
    scale = (64.0 * 4.0 * T) / total
    loads[-2].wait()
    loads[-1].wait()
    for i in (2, 3, 4):
        halo[i].wait_recv()
    last = tm == 63
    for b in range(5):
        rows = 128 if b < 4 else HALO
        lo = 128 * b
        weighting = jnp.broadcast_to(swe[:, lo:lo + 128] * scale, (128, 128)).T[:rows]
        if b == 4:
            weighting = jnp.where(last, 0.0, weighting)
        weighting = jnp.concatenate([weighting, weighting], axis=1)
        gs[lo:lo + rows] = gse[lo:lo + rows].astype(F32) * weighting
        gproj[lo:lo + rows, C:2 * C] = (gke[lo:lo + rows].astype(F32) * weighting).astype(BF16)

    copies = []
    pending = []

    def part_start(part, source):
        for half in range(2):
            for y in range(4):
                if part % 3 == 2:
                    if half == 1:
                        continue
                    tile = source[1 - at["core"], :, :, y * 128:(y + 1) * 128]
                    csend[part, y] = tile.reshape(4, 8, 8, 128).astype(BF16)
                else:
                    lo = (half * 4 + y) * 128
                    tile = source[:, pl.ds(1 - at["core"], 1), :, lo:lo + 128]
                    csend[part, y, 2 * half:2 * half + 2] = tile.reshape(2, 8, 8, 128).astype(BF16)
        copy = remote(
            csend.at[part], crecv.at[part], p_send.at[part, 0], p_recv.at[part, 0], device(peer(at, "core", 1))
        )
        copies.append(copy)
        return copy

    def part_join(part, source, copy):
        copy.wait_recv()
        for half in range(2):
            for y in range(4):
                if part % 3 == 2:
                    if half == 1:
                        continue
                    tile = source[at["core"], :, :, y * 128:(y + 1) * 128].reshape(4, 8, 8, 128)
                    hsum[part, y] = (tile + crecv[part, y].astype(F32)).astype(BF16)
                else:
                    lo = (half * 4 + y) * 128
                    tile = source[:, pl.ds(at["core"], 1), :, lo:lo + 128].reshape(2, 8, 8, 128)
                    rows = slice(2 * half, 2 * half + 2)
                    hsum[part, y, rows] = (tile + crecv[part, y, rows].astype(F32)).astype(BF16)
        stage_send(part, 0)

    def pick(ref, dims, axis, index):
        return ref.at[tuple(index if a == axis else slice(None) for a in dims)]

    def buffers(part, step):
        dims = [a for a in "yxz" if a not in ORDERS[part][:step]]
        source = hsum.at[part] if step == 0 else sums[2 * part + step - 1]
        return source, dims, landings[3 * part + step]

    def stage_send(part, step):
        axis = ORDERS[part][step]
        source, dims, landing = buffers(part, step)
        base = 1 + sum(SIZES[a] - 1 for a in ORDERS[part][:step])
        group = []
        for k in range(1, SIZES[axis]):
            other = peer(at, axis, k)
            copy = remote(
                pick(source, dims, axis, other[axis]), landing.at[k - 1],
                p_send.at[part, base + k - 1], p_recv.at[part, base + k - 1], device(other),
            )
            copies.append(copy)
            group.append(copy)
        pending.append((part, step, group))

    def stage_finish(part, step):
        entry = [e for e in pending if e[:2] == (part, step)][0]
        pending.remove(entry)
        axis = ORDERS[part][step]
        source, dims, landing = buffers(part, step)
        for copy in entry[2]:
            copy.wait_recv()
        total = pick(source, dims, axis, at[axis])[...].astype(F32)
        for k in range(SIZES[axis] - 1):
            total = total + landing[k].astype(F32)
        if step < 2:
            target, _, _ = buffers(part, step + 1)
            target[...] = total.astype(BF16)
            stage_send(part, step + 1)
        elif part % 3 == 2:
            high = LAYERS - 1 - 2 * (part // 3)
            gout_ref[high] = total[0:4]
            gout_ref[high - 1] = total[4:8]
        else:
            gconv_ref[LAYERS - 1 - 2 * (part // 3) - part % 3] = total

    gp[576:608] = jnp.zeros((32, 2 * C), F32)
    upper = lax.broadcasted_iota(jnp.int32, (32, 8, 2 * C), 1) < 4
    started = {}
    for l in reversed(range(LAYERS)):
        d = 2**l
        rows = BACK_ROWS[l]
        half_rows = 304 if rows > 560 else 272
        for r0, r1 in ((0, half_rows), (half_rows, rows)):
            gproj[r0:r1, 0:C] = gs[r0:r1].astype(BF16)
            grad_gated = contract_columns(gproj[r0:r1], outw[l])
            filtered, opening = filt_s[l, r0:r1], open_s[l, r0:r1]
            through = grad_gated * opening
            gp[r0:r1, 0:C] = through * (1.0 - filtered * filtered)
            gp[r0:r1, C:2 * C] = through * filtered * (1.0 - opening)
        pair = (LAYERS - 1 - l) // 2
        og[l % 2] = contract_rows(gated_s[l], gproj[0:T]).reshape(32, 8, 2 * C)
        if l % 2 == 0:
            high, low = og[1], og[0]
            shifted_low = pltpu.roll(low.reshape(256, 2 * C), 4, 0).reshape(32, 8, 2 * C)
            og2 = jnp.where(upper, high, shifted_low)
            shifted_high = pltpu.roll(high.reshape(256, 2 * C), 252, 0).reshape(32, 8, 2 * C)
            og[0] = og2
            og[1] = jnp.where(upper, shifted_high, low)
            part = 3 * pair + 2
            started[part] = part_start(part, og)
        update = BACK_ROWS[l - 1] if l else T
        gpb[0:rows] = gp[0:rows].astype(BF16)
        later_b[0:update] = gp[d:d + update].astype(BF16)
        part = 3 * pair + (1 - l % 2)
        mg[:, :, :, 0:2 * C] = contract_rows(pres_s[l], gpb[0:T]).reshape(16, 2, 8, 2 * C)
        mg[:, :, :, 2 * C:4 * C] = contract_rows(pres_s[l], later_b[0:T]).reshape(16, 2, 8, 2 * C)
        copy = part_start(part, mg)
        for r0, r1 in ((0, 256), (256, update)):
            taps = contract_columns(gpb[r0:r1], conv[l, 0:C]) + contract_columns(
                later_b[r0:r1], conv[l, C:2 * C]
            )
            grad_next = taps + gs[r0:r1]
            if l:
                gs[r0:r1] = grad_next
            else:
                gin_ref[0, r0:r1] = grad_next
        part_join(part, mg, copy)
        if l % 2 == 0:
            part_join(3 * pair + 2, og, started[3 * pair + 2])
        for part, step in SCHEDULE[l]:
            stage_finish(part, step)

    for copy in halo:
        copy.wait_send()
    for group, _, _ in wcopies:
        for copy in group:
            copy.wait_send()
    for copy in copies:
        copy.wait_send()


def body(inputs, grad_stream_out, grad_skip_out, sample_weight, conv_weight, out_weight):
    any_spec = pl.BlockSpec(memory_space=pl.ANY)
    vmem_spec = pl.BlockSpec(memory_space=pltpu.VMEM)
    landings, sums = [], []
    for order in ORDERS:
        for step in range(3):
            rest = tuple(SIZES[a] for a in "yxz" if a not in order[:step + 1])
            landings.append(pltpu.VMEM((SIZES[order[step]] - 1,) + rest + (8, 128), BF16))
            if step < 2:
                sums.append(pltpu.VMEM(rest + (8, 128), BF16))
    part_shape = (PARTS, 4, 4, 8, 8, 128)
    return pl.pallas_call(
        kernel,
        name="cycle",
        out_shape=(
            jax.ShapeDtypeStruct((1, T, C), F32),
            jax.ShapeDtypeStruct((LAYERS, 8, 128), F32),
            jax.ShapeDtypeStruct((LAYERS, 4, 128), F32),
        ),
        in_specs=[any_spec] * 6,
        out_specs=(vmem_spec, vmem_spec, vmem_spec),
        scratch_shapes=[
            pltpu.VMEM((EXT, C), BF16),
            pltpu.VMEM((POST, C), BF16),
            pltpu.VMEM((POST, C), BF16),
            pltpu.VMEM((1, T + 128), F32),
            pltpu.VMEM((LAYERS, 2 * C, 2 * C), BF16),
            pltpu.VMEM((LAYERS, C, 2 * C), BF16),
            pltpu.VMEM((32 + EXT, C), F32),
            pltpu.VMEM((LAYERS, T, C), BF16),
            pltpu.VMEM((LAYERS, T, C), BF16),
            pltpu.VMEM((LAYERS, POST, C), F32),
            pltpu.VMEM((LAYERS, POST, C), F32),
            pltpu.VMEM((POST, C), F32),
            pltpu.VMEM((POST, 2 * C), BF16),
            pltpu.VMEM((POST + 32, 2 * C), F32),
            pltpu.VMEM((POST, 2 * C), BF16),
            pltpu.VMEM((POST, 2 * C), BF16),
            pltpu.VMEM((16, 2, 8, 4 * C), F32),
            pltpu.VMEM((2, 32, 8, 2 * C), F32),
            pltpu.VMEM(part_shape, BF16),
            pltpu.VMEM(part_shape, BF16),
            pltpu.VMEM(part_shape, BF16),
            pltpu.VMEM((5, 8, 128), F32),
            pltpu.VMEM((14, 8, 128), F32),
            pltpu.SemaphoreType.DMA((16,)),
            pltpu.SemaphoreType.DMA((5,)),
            pltpu.SemaphoreType.DMA((5,)),
            pltpu.SemaphoreType.DMA((14,)),
            pltpu.SemaphoreType.DMA((14,)),
            pltpu.SemaphoreType.DMA((PARTS, 14)),
            pltpu.SemaphoreType.DMA((PARTS, 14)),
            *landings,
            *sums,
        ],
        compiler_params=pltpu.CompilerParams(
            collective_id=0, has_side_effects=True, vmem_limit_bytes=58 << 20
        ),
        cost_estimate=pl.CostEstimate(flops=8 * 10**9, bytes_accessed=8 * 10**6, transcendentals=4 * 10**6),
    )(inputs, grad_stream_out, grad_skip_out, sample_weight, conv_weight, out_weight)


def solution(mesh):
    placed = (
        P("dp", "tm", None),
        P("dp", "tm", None),
        P("dp", "tm", None),
        P("dp", "tm"),
        P(),
        P(),
    )
    return jax.shard_map(
        body,
        mesh=mesh,
        in_specs=placed,
        out_specs=(P("dp", "tm", None), P(None, "tm", "dp"), P(None, "tm", "dp")),
        check_vma=False,
    )
```

```python
import functools

import jax
import jax.numpy as jnp
from jax import lax
from jax.experimental import pallas as pl
from jax.experimental.pallas import tpu as pltpu
from jax.sharding import PartitionSpec as P

MESH = pl.DeviceIdType.MESH
F32, BF16 = jnp.float32, jnp.bfloat16
C, LAYERS, T, HALO = 256, 6, 512, 64
EXT = T + 2 * HALO
POST = T + HALO
SIZES = {"x": 4, "y": 4, "z": 8}
BACK_ROWS = (544, 544, 544, 544, 544, 576)
START = (0, 0, 0, 16, 32, 64)
FIRST = (80, 96, 112, 128, 144, 176)
MIDDLE = 336
BARRIER_AFTER = 3
PARTS = 9
ORDERS = ("yxz", "xyz", "zyx", "yxz", "xyz", "zyx", "yxz", "yxz", "xyz")

GROUPS = ((0, 1, 3, 4), (6, 7, 8), (2, 5))
TAIL = (
    (0, 0), (1, 0), (3, 0), (4, 0), (0, 1), (1, 1), (6, 0), (8, 0), (2, 0), (3, 1), (4, 1), "g0",
    (7, 0), (6, 1), (8, 1), (2, 1), (5, 0), (7, 1), "g1", (5, 1), "g2", "e0", "e1", "e2",
)


def contract_rows(left, right):
    return lax.dot_general(left, right, (((0,), (0,)), ((), ())), preferred_element_type=F32)


def contract_columns(left, right):
    return lax.dot_general(left, right, (((1,), (1,)), ((), ())), preferred_element_type=F32)


def place():
    tm, y = lax.axis_index("tm"), lax.axis_index("dp")
    return {"x": tm // 16, "y": y, "z": (tm // 2) % 8, "core": tm % 2}


def device(at):
    return ((at["x"] * 8 + at["z"]) * 2 + at["core"], at["y"])


def peer(at, axis, step):
    if axis == "core":
        return dict(at, core=1 - at["core"])
    return dict(at, **{axis: (at[axis] + step) % SIZES[axis]})


def remote(src, dst, send, recv, target):
    copy = pltpu.make_async_remote_copy(
        src_ref=src, dst_ref=dst, send_sem=send, recv_sem=recv,
        device_id=target, device_id_type=MESH,
    )
    copy.start()
    return copy


def kernel(
    x_hbm, gso_hbm, gsk_hbm, sw_hbm, conv_hbm, outw_hbm,
    gin_hbm, parts_ref,
    xe, gse, gke, swe, conv, outw,
    stream, tail_s, postb, pres_s, gated_s, filt_s, open_s,
    gs, gproj, gp, gpb, later_b, mg, og,
    csend, crecv, hsum, wtile, wrecv,
    load_sem, halo_send, halo_recv, w_send, w_recv, c_send, c_recv, s_send, s_recv, g_send, g_recv, out_sem, *rest,
):
    landings, sums, finals, final_in = rest[:18], rest[18:27], rest[27:30], rest[30:]
    at = place()
    tm = lax.axis_index("tm")
    nxt = ((tm + 1) % 64, at["y"])
    prv = ((tm + 63) % 64, at["y"])

    barrier = pltpu.get_barrier_semaphore()
    greet = [nxt, prv, device(peer(at, "core", 1))]
    for axis in "yxz":
        greet += [device(peer(at, axis, k)) for k in range(1, SIZES[axis])]
    for target in greet:
        pl.semaphore_signal(barrier, inc=1, device_id=target, device_id_type=MESH)

    loads = [
        pltpu.make_async_copy(x_hbm.at[0], xe.at[pl.ds(HALO, T)], load_sem.at[0]),
        pltpu.make_async_copy(sw_hbm, swe.at[:, pl.ds(0, T)], load_sem.at[1]),
    ]
    for l in range(LAYERS):
        loads.append(pltpu.make_async_copy(conv_hbm.at[l], conv.at[l], load_sem.at[4 + l]))
        loads.append(pltpu.make_async_copy(outw_hbm.at[l], outw.at[l], load_sem.at[10 + l]))
    loads.append(pltpu.make_async_copy(gso_hbm.at[0], gse.at[pl.ds(0, T)], load_sem.at[2]))
    loads.append(pltpu.make_async_copy(gsk_hbm.at[0], gke.at[pl.ds(0, T)], load_sem.at[3]))
    for copy in loads:
        copy.start()

    def activate(l, present, earlier):
        preact = jnp.dot(present, conv[l, 0:C], preferred_element_type=F32) + jnp.dot(
            earlier, conv[l, C:2 * C], preferred_element_type=F32
        )
        filtered = jnp.tanh(preact[:, :C])
        opening = 0.5 * jnp.tanh(0.5 * preact[:, C:]) + 0.5
        return filtered, opening, (filtered * opening).astype(BF16)

    loads[0].wait()
    stream[32 + HALO:32 + HALO + T] = xe[HALO:HALO + T].astype(F32)
    wcopies = []
    halo = []
    for l in range(LAYERS):
        d = 2**l
        loads[2 + 2 * l].wait()
        loads[3 + 2 * l].wait()
        tail_s[l] = stream[HALO + T:HALO + T + 32]
        for lo, hi in ((MIDDLE, HALO + T), (FIRST[l], MIDDLE)):
            present = stream[32 + lo:32 + hi].astype(BF16)
            filtered, opening, gated = activate(l, present, stream[32 + lo - d:32 + hi - d].astype(BF16))
            filt_s[l, lo - HALO:hi - HALO] = filtered
            open_s[l, lo - HALO:hi - HALO] = opening
            pres_s[l, lo - HALO:hi - HALO] = present
            gated_s[l, lo - HALO:hi - HALO] = gated
            if l < LAYERS - 1:
                stream[32 + lo:32 + hi] += jnp.dot(gated, outw[l, :, 0:C], preferred_element_type=F32)
        if l == BARRIER_AFTER:
            pl.semaphore_wait(barrier, len(greet))
            first, final = pl.ds(0, HALO), pl.ds(T, HALO)
            halo = [
                remote(x_hbm.at[0, pl.ds(T - HALO, HALO)], xe.at[first], halo_send.at[0], halo_recv.at[0], nxt),
                remote(x_hbm.at[0, first], xe.at[pl.ds(HALO + T, HALO)], halo_send.at[1], halo_recv.at[1], prv),
                remote(gso_hbm.at[0, first], gse.at[final], halo_send.at[2], halo_recv.at[2], prv),
                remote(gsk_hbm.at[0, first], gke.at[final], halo_send.at[3], halo_recv.at[3], prv),
                remote(sw_hbm.at[:, pl.ds(0, 128)], swe.at[:, pl.ds(T, 128)], halo_send.at[4], halo_recv.at[4], prv),
            ]

    loads[1].wait()
    wtile[0] = jnp.broadcast_to(
        swe[:, 0:128] + swe[:, 128:256] + swe[:, 256:384] + swe[:, 384:512], (8, 128)
    )

    def weight_send(step, axis, base):
        group = []
        for k in range(1, 2 if axis == "core" else SIZES[axis]):
            slot = base + k - 1
            group.append(remote(
                wtile.at[step], wrecv.at[slot], w_send.at[slot], w_recv.at[slot], device(peer(at, axis, k))
            ))
        wcopies.append((group, step, base))

    def weight_sum():
        group, step, base = wcopies[-1]
        total = wtile[step]
        for k, copy in enumerate(group):
            copy.wait_recv()
            total = total + wrecv[base + k]
        wtile[step + 1] = total

    weight_send(0, "core", 0)

    loads[-2].wait()
    loads[-1].wait()

    def weigh(b, rows):
        lo = 128 * b
        weighting = jnp.broadcast_to(swe[:, lo:lo + 128], (128, 128)).T[:rows]
        if lo == T:
            weighting = jnp.where(tm == 63, 0.0, weighting)
        weighting = jnp.concatenate([weighting, weighting], axis=1)
        gs[lo:lo + rows] = gse[lo:lo + rows].astype(F32) * weighting
        gproj[lo:lo + rows, C:2 * C] = (gke[lo:lo + rows].astype(F32) * weighting).astype(BF16)

    for b in range(4):
        weigh(b, 128)

    stream[0:32] = jnp.zeros((32, C), F32)
    halo[0].wait_recv()
    halo[1].wait_recv()
    stream[32:32 + HALO] = jnp.where(tm == 0, 0.0, xe[0:HALO].astype(F32))
    postb[32:96] = xe[HALO + T:].astype(F32)
    for l in range(LAYERS):
        d = 2**l
        lo, hi = START[l], FIRST[l]
        count = hi - lo
        postb[0:32] = tail_s[l]
        present = jnp.concatenate([stream[32 + lo:32 + hi], postb[32:96]], axis=0).astype(BF16)
        earlier = jnp.concatenate([stream[32 + lo - d:32 + hi - d], postb[32 - d:96 - d]], axis=0).astype(BF16)
        filtered, opening, gated = activate(l, present, earlier)
        skip = HALO - lo
        filt_s[l, 0:hi - HALO] = filtered[skip:count]
        open_s[l, 0:hi - HALO] = opening[skip:count]
        pres_s[l, 0:hi - HALO] = present[skip:count]
        gated_s[l, 0:hi - HALO] = gated[skip:count]
        filt_s[l, T:POST] = filtered[count:]
        open_s[l, T:POST] = opening[count:]
        if l < LAYERS - 1:
            projected = jnp.dot(gated, outw[l, :, 0:C], preferred_element_type=F32)
            stream[32 + lo:32 + hi] += projected[:count]
            postb[32:96] += projected[count:]
        if l == 1:
            weight_sum()
            weight_send(1, "y", 1)
    for i in (2, 3, 4):
        halo[i].wait_recv()
    weigh(4, HALO)

    copies = []
    pending = []

    def part_start(part, source):
        for half in range(2):
            for y in range(4):
                if part % 3 == 2:
                    if half == 1:
                        continue
                    tile = source[1 - at["core"], :, :, y * 128:(y + 1) * 128]
                    csend[part, y] = tile.reshape(4, 8, 8, 128).astype(BF16)
                else:
                    lo = (half * 4 + y) * 128
                    tile = source[:, pl.ds(1 - at["core"], 1), :, lo:lo + 128]
                    csend[part, y, 2 * half:2 * half + 2] = tile.reshape(2, 8, 8, 128).astype(BF16)
        copy = remote(
            csend.at[part], crecv.at[part], c_send.at[part], c_recv.at[part], device(peer(at, "core", 1))
        )
        copies.append(copy)
        return copy

    def part_join(part, source, copy):
        copy.wait_recv()
        for half in range(2):
            for y in range(4):
                if part % 3 == 2:
                    if half == 1:
                        continue
                    tile = source[at["core"], :, :, y * 128:(y + 1) * 128].reshape(4, 8, 8, 128)
                    hsum[part, y] = (tile + crecv[part, y].astype(F32)).astype(BF16)
                else:
                    lo = (half * 4 + y) * 128
                    tile = source[:, pl.ds(at["core"], 1), :, lo:lo + 128].reshape(2, 8, 8, 128)
                    rows = slice(2 * half, 2 * half + 2)
                    hsum[part, y, rows] = (tile + crecv[part, y, rows].astype(F32)).astype(BF16)
        stage_send(part, 0)

    def pick(ref, dims, axis, index):
        return ref.at[tuple(index if a == axis else slice(None) for a in dims)]

    def send_all(axis, pick_source, landing, send, recv):
        for k in range(1, SIZES[axis]):
            other = peer(at, axis, k)
            remote(pick_source(other[axis]), landing.at[k - 1], send, recv, device(other))
        waits.append((landing, send))

    def wait_all(landing, semaphore):
        pltpu.make_async_copy(landing, landing, semaphore).wait()

    def stage(part, step):
        dims = [a for a in "yxz" if a not in ORDERS[part][:step]]
        source = hsum.at[part] if step == 0 else sums[part]
        return ORDERS[part][step], dims, source, landings[2 * part + step]

    def stage_send(part, step):
        axis, dims, source, landing = stage(part, step)
        send_all(axis, lambda i: pick(source, dims, axis, i), landing, s_send.at[part, step], s_recv.at[part, step])

    def stage_finish(part, step):
        axis, dims, source, landing = stage(part, step)
        wait_all(landing, s_recv.at[part, step])
        total = pick(source, dims, axis, at[axis])[...].astype(F32)
        for k in range(SIZES[axis] - 1):
            total = total + landing[k].astype(F32)
        if step == 0:
            sums[part][...] = total.astype(BF16)
            stage_send(part, 1)
        else:
            g = [part in group for group in GROUPS].index(True)
            finals[g][:, GROUPS[g].index(part)] = total.astype(BF16)

    def group_send(g):
        send_all(ORDERS[GROUPS[g][0]][2], lambda i: finals[g].at[i], final_in[g], g_send.at[g], g_recv.at[g])

    def group_finish(g, scale):
        axis = ORDERS[GROUPS[g][0]][2]
        wait_all(final_in[g], g_recv.at[g])
        total = finals[g][at[axis]].astype(F32)
        for k in range(SIZES[axis] - 1):
            total = total + final_in[g][k].astype(F32)
        for j, part in enumerate(GROUPS[g]):
            parts_ref[part] = total[j] * scale

    waits = []
    gp[576:608] = jnp.zeros((32, 2 * C), F32)
    upper = lax.broadcasted_iota(jnp.int32, (32, 8, 2 * C), 1) < 4
    joins = []
    for l in reversed(range(LAYERS)):
        d = 2**l
        rows = BACK_ROWS[l]
        half_rows = 304 if rows > 560 else 272
        for r0, r1 in ((0, half_rows), (half_rows, rows)):
            gproj[r0:r1, 0:C] = gs[r0:r1].astype(BF16)
            grad_gated = contract_columns(gproj[r0:r1], outw[l])
            filtered, opening = filt_s[l, r0:r1], open_s[l, r0:r1]
            through = grad_gated * opening
            gp[r0:r1, 0:C] = through * (1.0 - filtered * filtered)
            gp[r0:r1, C:2 * C] = through * filtered * (1.0 - opening)
        for join in joins:
            part_join(*join)
        joins = []
        pair = (LAYERS - 1 - l) // 2
        update = BACK_ROWS[l - 1] if l else T
        gpb[0:rows] = gp[0:rows].astype(BF16)
        later_b[0:update] = gp[d:d + update].astype(BF16)
        part = 3 * pair + (1 - l % 2)
        mg[:, :, :, 0:2 * C] = contract_rows(pres_s[l], gpb[0:T]).reshape(16, 2, 8, 2 * C)
        mg[:, :, :, 2 * C:4 * C] = contract_rows(pres_s[l], later_b[0:T]).reshape(16, 2, 8, 2 * C)
        joins.append((part, mg, part_start(part, mg)))
        og[l % 2] = contract_rows(gated_s[l], gproj[0:T]).reshape(32, 8, 2 * C)
        if l % 2 == 0:
            high, low = og[1], og[0]
            shifted_low = pltpu.roll(low.reshape(256, 2 * C), 4, 0).reshape(32, 8, 2 * C)
            shifted_high = pltpu.roll(high.reshape(256, 2 * C), 252, 0).reshape(32, 8, 2 * C)
            og[0] = jnp.where(upper, high, shifted_low)
            og[1] = jnp.where(upper, shifted_high, low)
            part = 3 * pair + 2
            joins.append((part, og, part_start(part, og)))
        for r0, r1 in ((0, 256), (256, update)):
            taps = contract_columns(gpb[r0:r1], conv[l, 0:C]) + contract_columns(
                later_b[r0:r1], conv[l, C:2 * C]
            )
            grad_next = taps + gs[r0:r1]
            gs[r0:r1] = grad_next
        if l == 5:
            weight_sum()
            weight_send(2, "x", 4)
        if l == 2:
            weight_sum()
            weight_send(3, "z", 7)
    for join in joins:
        part_join(*join)
    for item in TAIL:
        if item == "g0":
            group_send(0)
            weight_sum()
            scale = (64.0 * 4.0 * T) / jnp.sum(wtile[4][0:1], axis=1, keepdims=True)
            gs[0:T] = gs[0:T] * scale
            out_copy = pltpu.make_async_copy(gs.at[pl.ds(0, T)], gin_hbm.at[0], out_sem)
            out_copy.start()
        elif item in ("g1", "g2"):
            group_send(int(item[1]))
        elif item in ("e0", "e1", "e2"):
            group_finish(int(item[1]), scale)
        else:
            stage_finish(*item)
    out_copy.wait()
    for landing, semaphore in waits:
        wait_all(landing, semaphore)

    for copy in halo:
        copy.wait_send()
    for group, _, _ in wcopies:
        for copy in group:
            copy.wait_send()
    for copy in copies:
        copy.wait_send()


def deliver(gin_ref, parts_ref, gin_out, gconv_out, gout_out):
    gin_out[...] = gin_ref[...]
    for part in range(PARTS):
        layer = LAYERS - 1 - 2 * (part // 3)
        if part % 3 == 2:
            gout_out[layer] = parts_ref[part, 0:4]
            gout_out[layer - 1] = parts_ref[part, 4:8]
        else:
            gconv_out[layer - part % 3] = parts_ref[part]


def body(inputs, grad_stream_out, grad_skip_out, sample_weight, conv_weight, out_weight):
    any_spec = pl.BlockSpec(memory_space=pl.ANY)
    vmem_spec = pl.BlockSpec(memory_space=pltpu.VMEM)
    landings, sums, finals, final_in = [], [], [], []
    for order in ORDERS:
        for step in range(2):
            rest = tuple(SIZES[a] for a in "yxz" if a not in order[:step + 1])
            landings.append(pltpu.VMEM((SIZES[order[step]] - 1,) + rest + (8, 128), BF16))
            if step == 0:
                sums.append(pltpu.VMEM(rest + (8, 128), BF16))
    for group in GROUPS:
        size = SIZES[ORDERS[group[0]][2]]
        finals.append(pltpu.VMEM((size, len(group), 8, 128), BF16))
        final_in.append(pltpu.VMEM((size - 1, len(group), 8, 128), BF16))
    part_shape = (PARTS, 4, 4, 8, 8, 128)
    gin, parts = pl.pallas_call(
        kernel,
        name="cycle",
        out_shape=(
            jax.ShapeDtypeStruct((1, T, C), F32),
            jax.ShapeDtypeStruct((PARTS, 8, 128), F32),
        ),
        in_specs=[any_spec] * 6,
        out_specs=(any_spec, vmem_spec),
        scratch_shapes=[
            pltpu.VMEM((EXT, C), BF16),
            pltpu.VMEM((POST, C), BF16),
            pltpu.VMEM((POST, C), BF16),
            pltpu.VMEM((1, T + 128), F32),
            pltpu.VMEM((LAYERS, 2 * C, 2 * C), BF16),
            pltpu.VMEM((LAYERS, C, 2 * C), BF16),
            pltpu.VMEM((32 + HALO + T, C), F32),
            pltpu.VMEM((LAYERS, 32, C), F32),
            pltpu.VMEM((96, C), F32),
            pltpu.VMEM((LAYERS, T, C), BF16),
            pltpu.VMEM((LAYERS, T, C), BF16),
            pltpu.VMEM((LAYERS, POST, C), F32),
            pltpu.VMEM((LAYERS, POST, C), F32),
            pltpu.VMEM((POST, C), F32),
            pltpu.VMEM((POST, 2 * C), BF16),
            pltpu.VMEM((POST + 32, 2 * C), F32),
            pltpu.VMEM((POST, 2 * C), BF16),
            pltpu.VMEM((POST, 2 * C), BF16),
            pltpu.VMEM((16, 2, 8, 4 * C), F32),
            pltpu.VMEM((2, 32, 8, 2 * C), F32),
            pltpu.VMEM(part_shape, BF16),
            pltpu.VMEM(part_shape, BF16),
            pltpu.VMEM(part_shape, BF16),
            pltpu.VMEM((5, 8, 128), F32),
            pltpu.VMEM((14, 8, 128), F32),
            pltpu.SemaphoreType.DMA((16,)),
            pltpu.SemaphoreType.DMA((5,)),
            pltpu.SemaphoreType.DMA((5,)),
            pltpu.SemaphoreType.DMA((14,)),
            pltpu.SemaphoreType.DMA((14,)),
            pltpu.SemaphoreType.DMA((PARTS,)),
            pltpu.SemaphoreType.DMA((PARTS,)),
            pltpu.SemaphoreType.DMA((PARTS, 2)),
            pltpu.SemaphoreType.DMA((PARTS, 2)),
            pltpu.SemaphoreType.DMA((3,)),
            pltpu.SemaphoreType.DMA((3,)),
            pltpu.SemaphoreType.DMA,
            *landings,
            *sums,
            *finals,
            *final_in,
        ],
        compiler_params=pltpu.CompilerParams(
            collective_id=0, has_side_effects=True, vmem_limit_bytes=58 << 20
        ),
        cost_estimate=pl.CostEstimate(flops=8 * 10**9, bytes_accessed=8 * 10**6, transcendentals=4 * 10**6),
    )(inputs, grad_stream_out, grad_skip_out, sample_weight, conv_weight, out_weight)
    return pl.pallas_call(
        deliver,
        name="deliver",
        out_shape=(
            jax.ShapeDtypeStruct((1, T, C), F32),
            jax.ShapeDtypeStruct((LAYERS, 8, 128), F32),
            jax.ShapeDtypeStruct((LAYERS, 4, 128), F32),
        ),
        in_specs=[vmem_spec, vmem_spec],
        out_specs=(vmem_spec, vmem_spec, vmem_spec),
    )(gin, parts)


def solution(mesh):
    placed = (
        P("dp", "tm", None),
        P("dp", "tm", None),
        P("dp", "tm", None),
        P("dp", "tm"),
        P(),
        P(),
    )
    return jax.shard_map(
        body,
        mesh=mesh,
        in_specs=placed,
        out_specs=(P("dp", "tm", None), P(None, "tm", "dp"), P(None, "tm", "dp")),
        check_vma=False,
    )
```

```python
import functools

import jax
import jax.numpy as jnp
from jax import lax
from jax.experimental import pallas as pl
from jax.experimental.pallas import tpu as pltpu
from jax.sharding import PartitionSpec as P

MESH = pl.DeviceIdType.MESH
F32, BF16 = jnp.float32, jnp.bfloat16
C, LAYERS, T, HALO = 256, 6, 512, 64
EXT = T + 2 * HALO
POST = T + HALO
SIZES = {"x": 4, "y": 4, "z": 8}
BACK_ROWS = (544, 544, 544, 544, 544, 576)
START = (0, 0, 0, 16, 32, 64)
FIRST = (80, 96, 112, 128, 144, 176)
MIDDLE = 336
BUFFERS = 17
CHUNKS = ((5,), (4, 3), (2, 1), (0,))
HALVED = (0, 1, 2)
INSIDE = {1: ((0, 0),)}
TAIL = (
    (1, 0), (0, 1), (2, 0), (1, 1), (0, 2), (3, 1), (2, 1), (1, 2), "scale", (0, 3), (3, 2), (2, 2), (1, 3), (3, 3),
    (2, 3),
)


def contract_rows(left, right):
    return lax.dot_general(left, right, (((0,), (0,)), ((), ())), preferred_element_type=F32)


def contract_columns(left, right):
    return lax.dot_general(left, right, (((1,), (1,)), ((), ())), preferred_element_type=F32)


def place():
    tm, y = lax.axis_index("tm"), lax.axis_index("dp")
    return {"x": tm // 16, "y": y, "z": (tm // 2) % 8, "core": tm % 2}


def device(at):
    return ((at["x"] * 8 + at["z"]) * 2 + at["core"], at["y"])


def flips(i):
    return (i + 1 - 2 * (i % 2), 3 - i), (3 - i, i + 1 - 2 * (i % 2))


def peer(at, axis, step):
    if axis == "core":
        return dict(at, core=1 - at["core"])
    return dict(at, **{axis: (at[axis] + step) % SIZES[axis]})


def remote(src, dst, send, recv, target):
    copy = pltpu.make_async_remote_copy(
        src_ref=src, dst_ref=dst, send_sem=send, recv_sem=recv,
        device_id=target, device_id_type=MESH,
    )
    copy.start()
    return copy


def kernel(
    x_hbm, gso_hbm, gsk_hbm, sw_hbm, conv_hbm, outw_hbm,
    gin_hbm, parts_ref,
    xe, gse, gke, swe, conv, outw,
    stream, tail_s, postb, pres_s, gated_s, filt_s, open_s,
    gs, gproj, gp, gpb, later_b, wtile, wrecv,
    load_sem, halo_send, halo_recv, w_send, w_recv, p_send, p_recv, out_sem, *rest,
):
    bufs = [rest[BUFFERS * i:BUFFERS * (i + 1)] for i in range(len(CHUNKS))]
    at = place()
    tm = lax.axis_index("tm")
    nxt = ((tm + 1) % 64, at["y"])
    prv = ((tm + 63) % 64, at["y"])

    barrier = pltpu.get_barrier_semaphore()
    greet = [nxt, prv, device(peer(at, "core", 1))]
    for axis in "yxz":
        greet += [device(peer(at, axis, k)) for k in range(1, SIZES[axis])]
    for target in greet:
        pl.semaphore_signal(barrier, inc=1, device_id=target, device_id_type=MESH)

    loads = [
        pltpu.make_async_copy(x_hbm.at[0], xe.at[pl.ds(HALO, T)], load_sem.at[0]),
        pltpu.make_async_copy(sw_hbm, swe.at[:, pl.ds(0, T)], load_sem.at[1]),
    ]
    for l in range(LAYERS):
        loads.append(pltpu.make_async_copy(conv_hbm.at[l], conv.at[l], load_sem.at[4 + l]))
        loads.append(pltpu.make_async_copy(outw_hbm.at[l], outw.at[l], load_sem.at[10 + l]))
    loads.append(pltpu.make_async_copy(gso_hbm.at[0], gse.at[pl.ds(0, T)], load_sem.at[2]))
    loads.append(pltpu.make_async_copy(gsk_hbm.at[0], gke.at[pl.ds(0, T)], load_sem.at[3]))
    for copy in loads[:6]:
        copy.start()

    pl.semaphore_wait(barrier, len(greet))
    first, final = pl.ds(0, HALO), pl.ds(T, HALO)
    halo = [
        remote(x_hbm.at[0, pl.ds(T - HALO, HALO)], xe.at[first], halo_send.at[0], halo_recv.at[0], nxt),
        remote(x_hbm.at[0, first], xe.at[pl.ds(HALO + T, HALO)], halo_send.at[1], halo_recv.at[1], prv),
        remote(gso_hbm.at[0, first], gse.at[final], halo_send.at[2], halo_recv.at[2], prv),
        remote(gsk_hbm.at[0, first], gke.at[final], halo_send.at[3], halo_recv.at[3], prv),
        remote(sw_hbm.at[:, pl.ds(0, 128)], swe.at[:, pl.ds(T, 128)], halo_send.at[4], halo_recv.at[4], prv),
    ]

    def activate(l, present, earlier):
        preact = jnp.dot(present, conv[l, 0:C], preferred_element_type=F32) + jnp.dot(
            earlier, conv[l, C:2 * C], preferred_element_type=F32
        )
        filtered = jnp.tanh(preact[:, :C])
        opening = 0.5 * jnp.tanh(0.5 * preact[:, C:]) + 0.5
        return filtered, opening, (filtered * opening).astype(BF16)

    loads[0].wait()
    stream[32 + HALO:32 + HALO + T] = xe[HALO:HALO + T].astype(F32)
    wcopies = []
    for l in range(LAYERS):
        d = 2**l
        loads[2 + 2 * l].wait()
        loads[3 + 2 * l].wait()
        for copy in loads[6 + 2 * l:8 + 2 * l]:
            copy.start()
        tail_s[l] = stream[HALO + T:HALO + T + 32]
        for lo, hi in ((MIDDLE, HALO + T), (FIRST[l], MIDDLE)):
            present = stream[32 + lo:32 + hi].astype(BF16)
            filtered, opening, gated = activate(l, present, stream[32 + lo - d:32 + hi - d].astype(BF16))
            filt_s[l, lo - HALO:hi - HALO] = filtered
            open_s[l, lo - HALO:hi - HALO] = opening
            pres_s[l, lo - HALO:hi - HALO] = present
            gated_s[l, lo - HALO:hi - HALO] = gated
            if l < LAYERS - 1:
                stream[32 + lo:32 + hi] += jnp.dot(gated, outw[l, :, 0:C], preferred_element_type=F32)

    loads[1].wait()
    wtile[0] = jnp.broadcast_to(
        swe[:, 0:128] + swe[:, 128:256] + swe[:, 256:384] + swe[:, 384:512], (8, 128)
    )

    def weight_send(step, axis, base):
        group = []
        for k in range(1, 2 if axis == "core" else SIZES[axis]):
            slot = base + k - 1
            group.append(remote(
                wtile.at[step], wrecv.at[slot], w_send.at[slot], w_recv.at[slot], device(peer(at, axis, k))
            ))
        wcopies.append((group, step, base))

    def weight_sum():
        group, step, base = wcopies[-1]
        total = wtile[step]
        for k, copy in enumerate(group):
            copy.wait_recv()
            total = total + wrecv[base + k]
        wtile[step + 1] = total

    weight_send(0, "core", 0)

    loads[-2].wait()
    loads[-1].wait()

    def weigh(b, rows):
        lo = 128 * b
        weighting = jnp.broadcast_to(swe[:, lo:lo + 128], (128, 128)).T[:rows]
        if lo == T:
            weighting = jnp.where(tm == 63, 0.0, weighting)
        weighting = jnp.concatenate([weighting, weighting], axis=1)
        gs[lo:lo + rows] = gse[lo:lo + rows].astype(F32) * weighting
        gproj[lo:lo + rows, C:2 * C] = (gke[lo:lo + rows].astype(F32) * weighting).astype(BF16)

    for b in range(4):
        weigh(b, 128)

    stream[0:32] = jnp.zeros((32, C), F32)
    halo[0].wait_recv()
    halo[1].wait_recv()
    stream[32:32 + HALO] = jnp.where(tm == 0, 0.0, xe[0:HALO].astype(F32))
    postb[32:96] = xe[HALO + T:].astype(F32)
    for l in range(LAYERS):
        d = 2**l
        lo, hi = START[l], FIRST[l]
        count = hi - lo
        postb[0:32] = tail_s[l]
        present = jnp.concatenate([stream[32 + lo:32 + hi], postb[32:96]], axis=0).astype(BF16)
        earlier = jnp.concatenate([stream[32 + lo - d:32 + hi - d], postb[32 - d:96 - d]], axis=0).astype(BF16)
        filtered, opening, gated = activate(l, present, earlier)
        skip = HALO - lo
        filt_s[l, 0:hi - HALO] = filtered[skip:count]
        open_s[l, 0:hi - HALO] = opening[skip:count]
        pres_s[l, 0:hi - HALO] = present[skip:count]
        gated_s[l, 0:hi - HALO] = gated[skip:count]
        filt_s[l, T:POST] = filtered[count:]
        open_s[l, T:POST] = opening[count:]
        if l < LAYERS - 1:
            projected = jnp.dot(gated, outw[l, :, 0:C], preferred_element_type=F32)
            stream[32 + lo:32 + hi] += projected[:count]
            postb[32:96] += projected[count:]
        if l == 1:
            weight_sum()
            weight_send(1, "y", 1)
    for i in (2, 3, 4):
        halo[i].wait_recv()
    weigh(4, HALO)

    waits = []

    def send_all(axis, pick_source, landing, send, recv):
        for k in range(1, SIZES[axis]):
            other = peer(at, axis, k)
            remote(pick_source(other[axis]), landing.at[k - 1], send, recv, device(other))
        waits.append((landing, send))

    def wait_all(landing, semaphore):
        pltpu.make_async_copy(landing, landing, semaphore).wait()

    def collect(own, landing):
        low = own.astype(F32) + landing[0].astype(F32)
        return low + (landing[1].astype(F32) + landing[2].astype(F32))

    def chunk_join(i):
        grads, other, held, y_in, x_in = bufs[i][:5]
        wait_all(other, p_recv.at[i, 0])
        held[...] = grads[at["core"]] + other[...]
        if i in HALVED:
            for k, axis in enumerate("yx"):
                for half, (target, _) in enumerate(flips(at[axis])):
                    for slot, block in enumerate((target, (at[axis] + 2) % 4)):
                        remote(
                            held.at[quarter(axis, block, half)], bufs[i][11 + k].at[half, slot],
                            p_send.at[i, 1 + k], p_recv.at[i, 1 + k], device(dict(at, **{axis: target})),
                        )
                waits.append((bufs[i][11 + k], p_send.at[i, 1 + k]))
            return
        send_all("y", lambda y: held.at[y, :, :, pl.ds(0, 3)], y_in, p_send.at[i, 1], p_recv.at[i, 1])
        send_all("x", lambda x: held.at[:, x, :, pl.ds(3, 3)], x_in, p_send.at[i, 2], p_recv.at[i, 2])

    def quarter(axis, block, half):
        rest = pl.ds(2 * half, 2)
        if axis == "y":
            return block, rest, slice(None), pl.ds(0, 3)
        return rest, block, slice(None), pl.ds(3, 3)

    def stage0(i):
        held = bufs[i][2]
        for k, axis in enumerate("yx"):
            arrived, kept, final_in = bufs[i][11 + k], bufs[i][13 + k], bufs[i][15 + k]
            wait_all(arrived, p_recv.at[i, 1 + k])
            for half, (_, target) in enumerate(flips(at[axis])):
                kept[half] = held[quarter(axis, target, half)] + arrived[half, 1]
                remote(
                    kept.at[half], final_in.at[half], p_send.at[i, 6 + k], p_recv.at[i, 6 + k],
                    device(dict(at, **{axis: target})),
                )
            waits.append((final_in, p_send.at[i, 6 + k]))

    def halved_sum(i, k):
        axis = "yx"[k]
        held, arrived, final_in, total = bufs[i][2], bufs[i][11 + k], bufs[i][15 + k], bufs[i][5 + k]
        wait_all(final_in, p_recv.at[i, 6 + k])
        for half in range(2):
            own = held[quarter(axis, at[axis], half)].astype(F32) + arrived[half, 0].astype(F32)
            total[2 * half:2 * half + 2] = (own + final_in[half].astype(F32)).astype(BF16)

    def stage1(i):
        held, y_in, x_in, y_sum, x_sum, yx_in, xy_in = bufs[i][2:9]
        if i in HALVED:
            halved_sum(i, 0)
        else:
            wait_all(y_in, p_recv.at[i, 1])
            y_sum[...] = collect(held[at["y"], :, :, 0:3], y_in).astype(BF16)
        send_all("x", lambda x: y_sum.at[x], yx_in, p_send.at[i, 3], p_recv.at[i, 3])
        if i in HALVED:
            halved_sum(i, 1)
        else:
            wait_all(x_in, p_recv.at[i, 2])
            x_sum[...] = collect(held[:, at["x"], :, 3:6], x_in).astype(BF16)
        send_all("y", lambda y: x_sum.at[y], xy_in, p_send.at[i, 4], p_recv.at[i, 4])

    mine = at["z"] // 4 == at["core"]

    def stage2(i):
        y_sum, x_sum, yx_in, xy_in, last_out, last_in = bufs[i][5:11]
        wait_all(yx_in, p_recv.at[i, 3])
        tiles = [collect(y_sum[at["x"]], yx_in)]
        wait_all(xy_in, p_recv.at[i, 4])
        tiles.append(collect(x_sum[at["y"]], xy_in))
        for j in range(4):
            rows = tiles[j // 3][:, j % 3]
            out_rows = tiles[1][:, 1 + j // 2, 8 * (j % 2):8 * (j % 2) + 8]
            for c in range(2):
                last_out[j, c] = jnp.concatenate([rows[:, 8 * c:8 * c + 8], out_rows], axis=1).astype(BF16)
        for j in range(4):
            for c in range(2):
                z = 4 * at["core"] + j
                here = jnp.logical_and(z == at["z"], c == at["core"])
                source, target = last_out.at[j, c], last_in.at[at["z"]]

                @pl.when(jnp.logical_not(here))
                def _():
                    remote(source, target, p_send.at[i, 5], p_recv.at[i, 5], device(dict(at, z=z, core=c)))

                @pl.when(here)
                def _():
                    pltpu.make_async_copy(source, target, p_recv.at[i, 5]).start()

    def stage3(i, scale):
        last_in = bufs[i][10]
        wait_all(last_in, p_recv.at[i, 5])
        total = last_in[0].astype(F32)
        for k in range(1, 8):
            total = total + last_in[k].astype(F32)
        total = total * scale
        for j, l in enumerate(CHUNKS[i]):
            parts_ref[l] = total[j]

    gp[576:608] = jnp.zeros((32, 2 * C), F32)
    joins = []
    for l in reversed(range(LAYERS)):
        d = 2**l
        rows = BACK_ROWS[l]
        half_rows = 304 if rows > 560 else 272
        for r0, r1 in ((0, half_rows), (half_rows, rows)):
            gproj[r0:r1, 0:C] = gs[r0:r1].astype(BF16)
            grad_gated = contract_columns(gproj[r0:r1], outw[l])
            filtered, opening = filt_s[l, r0:r1], open_s[l, r0:r1]
            through = grad_gated * opening
            gp[r0:r1, 0:C] = through * (1.0 - filtered * filtered)
            gp[r0:r1, C:2 * C] = through * filtered * (1.0 - opening)
        ready, joins = joins, []
        update = BACK_ROWS[l - 1] if l else T
        gpb[0:rows] = gp[0:rows].astype(BF16)
        later_b[0:update] = gp[d:d + update].astype(BF16)
        i = [l in chunk for chunk in CHUNKS].index(True)
        grads, j = bufs[i][0], CHUNKS[i].index(l)
        products = (
            contract_rows(pres_s[l], gpb[0:T]),
            contract_rows(pres_s[l], later_b[0:T]),
            contract_rows(gated_s[l], gproj[0:T]),
        )
        for half in range(2):
            for y in range(4):
                for k in range(2):
                    tile = products[k][:, y * 128:(y + 1) * 128].astype(BF16).reshape(2, 2, 4, 16, 128)
                    grads[half, y, 2 * k:2 * k + 2, j, 0:4] = tile[:, half]
                tile = products[2][:, y * 128:(y + 1) * 128].astype(BF16).reshape(4, 2, 2, 16, 128)
                grads[half, y, :, j, 4:6] = tile[:, half]
        if l == CHUNKS[i][-1]:
            remote(
                grads.at[1 - at["core"]], bufs[i][1], p_send.at[i, 0], p_recv.at[i, 0], device(peer(at, "core", 1))
            )
            waits.append((bufs[i][1], p_send.at[i, 0]))
            joins.append(i)
        for r0, r1 in ((0, 256), (256, update)):
            taps = contract_columns(gpb[r0:r1], conv[l, 0:C]) + contract_columns(
                later_b[r0:r1], conv[l, C:2 * C]
            )
            gs[r0:r1] = taps + gs[r0:r1]
        for i in ready:
            chunk_join(i)
        for i, _ in INSIDE.get(l, ()):
            stage0(i)
        if l == 3:
            weight_sum()
            weight_send(2, "x", 4)
        if l == 0:
            weight_sum()
            weight_send(3, "z", 7)
    for i in joins:
        chunk_join(i)
    scale = None
    for item in TAIL:
        if item == "scale":
            weight_sum()
            scale = (64.0 * 4.0 * T) / jnp.sum(wtile[4][0:1], axis=1, keepdims=True)
            gs[0:T] = gs[0:T] * scale
            out_copy = pltpu.make_async_copy(gs.at[pl.ds(0, T)], gin_hbm.at[0], out_sem)
            out_copy.start()
        elif item[1] == 0:
            stage0(item[0])
        elif item[1] == 1:
            stage1(item[0])
        elif item[1] == 2:
            stage2(item[0])
        else:
            stage3(item[0], scale)
    out_copy.wait()
    for landing, semaphore in waits:
        wait_all(landing, semaphore)
    for i in range(len(CHUNKS)):
        last_in = bufs[i][10]

        @pl.when(mine)
        def _():
            wait_all(last_in.at[pl.ds(0, 7)], p_send.at[i, 5])

        @pl.when(jnp.logical_not(mine))
        def _():
            wait_all(last_in, p_send.at[i, 5])

    for copy in halo:
        copy.wait_send()
    for group, _, _ in wcopies:
        for copy in group:
            copy.wait_send()


def deliver(gin_ref, parts_ref, gin_out, gconv_out, gout_out):
    gin_out[...] = gin_ref[...]
    core = lax.axis_index("tm") % 2
    gconv_out[...] = parts_ref[:, 0:8]
    gout_out[...] = jnp.where(core == 0, parts_ref[:, 8:12], parts_ref[:, 12:16])


def body(inputs, grad_stream_out, grad_skip_out, sample_weight, conv_weight, out_weight):
    any_spec = pl.BlockSpec(memory_space=pl.ANY)
    vmem_spec = pl.BlockSpec(memory_space=pltpu.VMEM)
    buffers = []
    for chunk in CHUNKS:
        n = len(chunk)
        shapes = (
            (2, 4, 4, n, 6), (4, 4, n, 6), (4, 4, n, 6), (3, 4, n, 3), (3, 4, n, 3), (4, n, 3), (4, n, 3),
            (3, n, 3), (3, n, 3), (4, 2, n), (8, n), (2, 2, 2, n, 3), (2, 2, 2, n, 3),
            (2, 2, n, 3), (2, 2, n, 3), (2, 2, n, 3), (2, 2, n, 3),
        )
        buffers += [pltpu.VMEM(shape + (16, 128), BF16) for shape in shapes]
    gin, parts = pl.pallas_call(
        kernel,
        name="cycle",
        out_shape=(
            jax.ShapeDtypeStruct((1, T, C), F32),
            jax.ShapeDtypeStruct((LAYERS, 16, 128), F32),
        ),
        in_specs=[any_spec] * 6,
        out_specs=(any_spec, vmem_spec),
        scratch_shapes=[
            pltpu.VMEM((EXT, C), BF16),
            pltpu.VMEM((POST, C), BF16),
            pltpu.VMEM((POST, C), BF16),
            pltpu.VMEM((1, T + 128), F32),
            pltpu.VMEM((LAYERS, 2 * C, 2 * C), BF16),
            pltpu.VMEM((LAYERS, C, 2 * C), BF16),
            pltpu.VMEM((32 + HALO + T, C), F32),
            pltpu.VMEM((LAYERS, 32, C), F32),
            pltpu.VMEM((96, C), F32),
            pltpu.VMEM((LAYERS, T, C), BF16),
            pltpu.VMEM((LAYERS, T, C), BF16),
            pltpu.VMEM((LAYERS, POST, C), F32),
            pltpu.VMEM((LAYERS, POST, C), F32),
            pltpu.VMEM((POST, C), F32),
            pltpu.VMEM((POST, 2 * C), BF16),
            pltpu.VMEM((POST + 32, 2 * C), F32),
            pltpu.VMEM((POST, 2 * C), BF16),
            pltpu.VMEM((POST, 2 * C), BF16),
            pltpu.VMEM((5, 8, 128), F32),
            pltpu.VMEM((14, 8, 128), F32),
            pltpu.SemaphoreType.DMA((16,)),
            pltpu.SemaphoreType.DMA((5,)),
            pltpu.SemaphoreType.DMA((5,)),
            pltpu.SemaphoreType.DMA((14,)),
            pltpu.SemaphoreType.DMA((14,)),
            pltpu.SemaphoreType.DMA((len(CHUNKS), 8)),
            pltpu.SemaphoreType.DMA((len(CHUNKS), 8)),
            pltpu.SemaphoreType.DMA,
            *buffers,
        ],
        compiler_params=pltpu.CompilerParams(
            collective_id=0, has_side_effects=True, vmem_limit_bytes=58 << 20
        ),
        cost_estimate=pl.CostEstimate(flops=8 * 10**9, bytes_accessed=8 * 10**6, transcendentals=4 * 10**6),
    )(inputs, grad_stream_out, grad_skip_out, sample_weight, conv_weight, out_weight)
    return pl.pallas_call(
        deliver,
        name="deliver",
        out_shape=(
            jax.ShapeDtypeStruct((1, T, C), F32),
            jax.ShapeDtypeStruct((LAYERS, 8, 128), F32),
            jax.ShapeDtypeStruct((LAYERS, 4, 128), F32),
        ),
        in_specs=[vmem_spec, vmem_spec],
        out_specs=(vmem_spec, vmem_spec, vmem_spec),
    )(gin, parts)


def solution(mesh):
    placed = (
        P("dp", "tm", None),
        P("dp", "tm", None),
        P("dp", "tm", None),
        P("dp", "tm"),
        P(),
        P(),
    )
    return jax.shard_map(
        body,
        mesh=mesh,
        in_specs=placed,
        out_specs=(P("dp", "tm", None), P(None, "tm", "dp"), P(None, "tm", "dp")),
        check_vma=False,
    )
```

```python
import functools

import jax
import jax.numpy as jnp
from jax import lax
from jax.experimental import pallas as pl
from jax.experimental.pallas import tpu as pltpu
from jax.sharding import PartitionSpec as P

MESH = pl.DeviceIdType.MESH
F32, BF16 = jnp.float32, jnp.bfloat16
C, LAYERS, T, HALO = 256, 6, 512, 64
EXT = T + 2 * HALO
POST = T + HALO
SIZES = {"x": 4, "y": 4, "z": 8}
BACK_ROWS = (544, 544, 544, 544, 544, 576)
START = (0, 0, 0, 16, 32, 64)
FIRST = (80, 96, 112, 128, 144, 176)
MIDDLE = 336
BUFFERS = 17
CHUNKS = ((5,), (4, 3), (2, 1), (0,))
HALVED = (0, 1, 2)
INSIDE = {1: ((0, 0),), 0: ((1, 0), (0, 1))}
TAIL = (
    "x", (2, 0), (1, 1), (0, 2), "z", (3, 1), (2, 1), (1, 2), (3, 2), (2, 2), "scale", (0, 3), (1, 3),
    (3, 3), (2, 3),
)


def contract_rows(left, right):
    return lax.dot_general(left, right, (((0,), (0,)), ((), ())), preferred_element_type=F32)


def contract_columns(left, right):
    return lax.dot_general(left, right, (((1,), (1,)), ((), ())), preferred_element_type=F32)


def place():
    tm, y = lax.axis_index("tm"), lax.axis_index("dp")
    return {"x": tm // 16, "y": y, "z": (tm // 2) % 8, "core": tm % 2}


def device(at):
    return ((at["x"] * 8 + at["z"]) * 2 + at["core"], at["y"])


def flips(i):
    return (i + 1 - 2 * (i % 2), 3 - i), (3 - i, i + 1 - 2 * (i % 2))


def peer(at, axis, step):
    if axis == "core":
        return dict(at, core=1 - at["core"])
    return dict(at, **{axis: (at[axis] + step) % SIZES[axis]})


def remote(src, dst, send, recv, target):
    copy = pltpu.make_async_remote_copy(
        src_ref=src, dst_ref=dst, send_sem=send, recv_sem=recv,
        device_id=target, device_id_type=MESH,
    )
    copy.start()
    return copy


def kernel(
    x_hbm, gso_hbm, gsk_hbm, sw_hbm, conv_hbm, outw_hbm,
    gin_hbm, parts_ref,
    xe, gse, gke, swe, conv, outw,
    stream, tail_s, postb, pres_s, gated_s, filt_s, open_s,
    gs, gproj, gp, gpb, later_b, wtile, wrecv,
    load_sem, halo_send, halo_recv, w_send, w_recv, p_send, p_recv, out_sem, known, *rest,
):
    bufs = [rest[BUFFERS * i:BUFFERS * (i + 1)] for i in range(len(CHUNKS))]
    at = place()
    tm = lax.axis_index("tm")
    nxt = ((tm + 1) % 64, at["y"])
    prv = ((tm + 63) % 64, at["y"])

    barrier = pltpu.get_barrier_semaphore()
    greet = [nxt, prv, device(peer(at, "core", 1))]
    for axis in "yxz":
        greet += [device(peer(at, axis, 1)), device(peer(at, axis, SIZES[axis] - 1))]
    for target in greet:
        pl.semaphore_signal(barrier, inc=1, device_id=target, device_id_type=MESH)

    loads = [
        pltpu.make_async_copy(x_hbm.at[0], xe.at[pl.ds(HALO, T)], load_sem.at[0]),
        pltpu.make_async_copy(sw_hbm, swe.at[:, pl.ds(0, T)], load_sem.at[1]),
    ]
    for l in range(LAYERS):
        loads.append(pltpu.make_async_copy(conv_hbm.at[l], conv.at[l], load_sem.at[4 + l]))
        loads.append(pltpu.make_async_copy(outw_hbm.at[l], outw.at[l], load_sem.at[10 + l]))
    loads.append(pltpu.make_async_copy(gso_hbm.at[0], gse.at[pl.ds(0, T)], load_sem.at[2]))
    loads.append(pltpu.make_async_copy(gsk_hbm.at[0], gke.at[pl.ds(0, T)], load_sem.at[3]))
    for copy in loads[:6]:
        copy.start()

    pl.semaphore_wait(barrier, len(greet))

    def tell(step):
        for k in (1, SIZES["z"] - 1):
            pl.semaphore_signal(known.at[step], inc=1, device_id=device(peer(at, "z", k)), device_id_type=MESH)

    def hear(step):
        pl.semaphore_wait(known.at[step], 2)

    tell(0)
    first, final = pl.ds(0, HALO), pl.ds(T, HALO)
    halo = [
        remote(x_hbm.at[0, pl.ds(T - HALO, HALO)], xe.at[first], halo_send.at[0], halo_recv.at[0], nxt),
        remote(x_hbm.at[0, first], xe.at[pl.ds(HALO + T, HALO)], halo_send.at[1], halo_recv.at[1], prv),
        remote(gso_hbm.at[0, first], gse.at[final], halo_send.at[2], halo_recv.at[2], prv),
        remote(gsk_hbm.at[0, first], gke.at[final], halo_send.at[3], halo_recv.at[3], prv),
        remote(sw_hbm.at[:, pl.ds(0, 128)], swe.at[:, pl.ds(T, 128)], halo_send.at[4], halo_recv.at[4], prv),
    ]

    def activate(l, present, earlier):
        preact = jnp.dot(present, conv[l, 0:C], preferred_element_type=F32) + jnp.dot(
            earlier, conv[l, C:2 * C], preferred_element_type=F32
        )
        filtered = jnp.tanh(preact[:, :C])
        opening = 0.5 * jnp.tanh(0.5 * preact[:, C:]) + 0.5
        return filtered, opening, (filtered * opening).astype(BF16)

    loads[0].wait()
    stream[32 + HALO:32 + HALO + T] = xe[HALO:HALO + T].astype(F32)
    wcopies = []
    for l in range(LAYERS):
        d = 2**l
        loads[2 + 2 * l].wait()
        loads[3 + 2 * l].wait()
        for copy in loads[6 + 2 * l:8 + 2 * l]:
            copy.start()
        tail_s[l] = stream[HALO + T:HALO + T + 32]
        for lo, hi in ((MIDDLE, HALO + T), (FIRST[l], MIDDLE)):
            present = stream[32 + lo:32 + hi].astype(BF16)
            filtered, opening, gated = activate(l, present, stream[32 + lo - d:32 + hi - d].astype(BF16))
            filt_s[l, lo - HALO:hi - HALO] = filtered
            open_s[l, lo - HALO:hi - HALO] = opening
            pres_s[l, lo - HALO:hi - HALO] = present
            gated_s[l, lo - HALO:hi - HALO] = gated
            if l < LAYERS - 1:
                stream[32 + lo:32 + hi] += jnp.dot(gated, outw[l, :, 0:C], preferred_element_type=F32)

    loads[1].wait()
    wtile[0] = jnp.broadcast_to(
        swe[:, 0:128] + swe[:, 128:256] + swe[:, 256:384] + swe[:, 384:512], (8, 128)
    )

    def weight_send(step, axis, base):
        group = []
        for k in range(1, 2 if axis == "core" else SIZES[axis]):
            slot = base + k - 1
            group.append(remote(
                wtile.at[step], wrecv.at[slot], w_send.at[slot], w_recv.at[slot], device(peer(at, axis, k))
            ))
        wcopies.append((group, step, base))

    def weight_sum():
        group, step, base = wcopies[-1]
        total = wtile[step]
        for k, copy in enumerate(group):
            copy.wait_recv()
            total = total + wrecv[base + k]
        wtile[step + 1] = total

    weight_send(0, "core", 0)

    loads[-2].wait()
    loads[-1].wait()

    def weigh(b, rows):
        lo = 128 * b
        weighting = jnp.broadcast_to(swe[:, lo:lo + 128], (128, 128)).T[:rows]
        if lo == T:
            weighting = jnp.where(tm == 63, 0.0, weighting)
        weighting = jnp.concatenate([weighting, weighting], axis=1)
        gs[lo:lo + rows] = gse[lo:lo + rows].astype(F32) * weighting
        gproj[lo:lo + rows, C:2 * C] = (gke[lo:lo + rows].astype(F32) * weighting).astype(BF16)

    for b in range(4):
        weigh(b, 128)

    stream[0:32] = jnp.zeros((32, C), F32)
    halo[0].wait_recv()
    halo[1].wait_recv()
    stream[32:32 + HALO] = jnp.where(tm == 0, 0.0, xe[0:HALO].astype(F32))
    postb[32:96] = xe[HALO + T:].astype(F32)
    for l in range(LAYERS):
        d = 2**l
        lo, hi = START[l], FIRST[l]
        count = hi - lo
        postb[0:32] = tail_s[l]
        present = jnp.concatenate([stream[32 + lo:32 + hi], postb[32:96]], axis=0).astype(BF16)
        earlier = jnp.concatenate([stream[32 + lo - d:32 + hi - d], postb[32 - d:96 - d]], axis=0).astype(BF16)
        filtered, opening, gated = activate(l, present, earlier)
        skip = HALO - lo
        filt_s[l, 0:hi - HALO] = filtered[skip:count]
        open_s[l, 0:hi - HALO] = opening[skip:count]
        pres_s[l, 0:hi - HALO] = present[skip:count]
        gated_s[l, 0:hi - HALO] = gated[skip:count]
        filt_s[l, T:POST] = filtered[count:]
        open_s[l, T:POST] = opening[count:]
        if l < LAYERS - 1:
            projected = jnp.dot(gated, outw[l, :, 0:C], preferred_element_type=F32)
            stream[32 + lo:32 + hi] += projected[:count]
            postb[32:96] += projected[count:]
    for i in (2, 3, 4):
        halo[i].wait_recv()
    hear(0)
    tell(1)
    weigh(4, HALO)

    waits = []

    def send_all(axis, pick_source, landing, send, recv):
        for k in range(1, SIZES[axis]):
            other = peer(at, axis, k)
            remote(pick_source(other[axis]), landing.at[k - 1], send, recv, device(other))
        waits.append((landing, send))

    def wait_all(landing, semaphore):
        pltpu.make_async_copy(landing, landing, semaphore).wait()

    def collect(own, landing):
        low = own.astype(F32) + landing[0].astype(F32)
        return low + (landing[1].astype(F32) + landing[2].astype(F32))

    def chunk_join(i):
        grads, other, held, y_in, x_in = bufs[i][:5]
        wait_all(other, p_recv.at[i, 0])
        held[...] = grads[at["core"]] + other[...]
        if i in HALVED:
            for k, axis in enumerate("yx"):
                for half, (target, _) in enumerate(flips(at[axis])):
                    for slot, block in enumerate((target, (at[axis] + 2) % 4)):
                        remote(
                            held.at[quarter(axis, block, half)], bufs[i][11 + k].at[half, slot],
                            p_send.at[i, 1 + k], p_recv.at[i, 1 + k], device(dict(at, **{axis: target})),
                        )
                waits.append((bufs[i][11 + k], p_send.at[i, 1 + k]))
            return
        send_all("y", lambda y: held.at[y, :, :, pl.ds(0, 3)], y_in, p_send.at[i, 1], p_recv.at[i, 1])
        send_all("x", lambda x: held.at[:, x, :, pl.ds(3, 3)], x_in, p_send.at[i, 2], p_recv.at[i, 2])

    def quarter(axis, block, half):
        rest = pl.ds(2 * half, 2)
        if axis == "y":
            return block, rest, slice(None), pl.ds(0, 3)
        return rest, block, slice(None), pl.ds(3, 3)

    def stage0(i):
        held = bufs[i][2]
        for k, axis in enumerate("yx"):
            arrived, kept, final_in = bufs[i][11 + k], bufs[i][13 + k], bufs[i][15 + k]
            wait_all(arrived, p_recv.at[i, 1 + k])
            for half, (_, target) in enumerate(flips(at[axis])):
                kept[half] = held[quarter(axis, target, half)] + arrived[half, 1]
                remote(
                    kept.at[half], final_in.at[half], p_send.at[i, 6 + k], p_recv.at[i, 6 + k],
                    device(dict(at, **{axis: target})),
                )
            waits.append((final_in, p_send.at[i, 6 + k]))

    def halved_sum(i, k):
        axis = "yx"[k]
        held, arrived, final_in, total = bufs[i][2], bufs[i][11 + k], bufs[i][15 + k], bufs[i][5 + k]
        wait_all(final_in, p_recv.at[i, 6 + k])
        for half in range(2):
            own = held[quarter(axis, at[axis], half)].astype(F32) + arrived[half, 0].astype(F32)
            total[2 * half:2 * half + 2] = (own + final_in[half].astype(F32)).astype(BF16)

    def stage1(i):
        held, y_in, x_in, y_sum, x_sum, yx_in, xy_in = bufs[i][2:9]
        if i in HALVED:
            halved_sum(i, 0)
        else:
            wait_all(y_in, p_recv.at[i, 1])
            y_sum[...] = collect(held[at["y"], :, :, 0:3], y_in).astype(BF16)
        send_all("x", lambda x: y_sum.at[x], yx_in, p_send.at[i, 3], p_recv.at[i, 3])
        if i in HALVED:
            halved_sum(i, 1)
        else:
            wait_all(x_in, p_recv.at[i, 2])
            x_sum[...] = collect(held[:, at["x"], :, 3:6], x_in).astype(BF16)
        send_all("y", lambda y: x_sum.at[y], xy_in, p_send.at[i, 4], p_recv.at[i, 4])

    mine = at["z"] // 4 == at["core"]

    def stage2(i):
        y_sum, x_sum, yx_in, xy_in, last_out, last_in = bufs[i][5:11]
        wait_all(yx_in, p_recv.at[i, 3])
        tiles = [collect(y_sum[at["x"]], yx_in)]
        wait_all(xy_in, p_recv.at[i, 4])
        tiles.append(collect(x_sum[at["y"]], xy_in))
        for j in range(4):
            rows = tiles[j // 3][:, j % 3]
            out_rows = tiles[1][:, 1 + j // 2, 8 * (j % 2):8 * (j % 2) + 8]
            for c in range(2):
                last_out[j, c] = jnp.concatenate([rows[:, 8 * c:8 * c + 8], out_rows], axis=1).astype(BF16)
        for j in range(4):
            for c in range(2):
                z = 4 * at["core"] + j
                here = jnp.logical_and(z == at["z"], c == at["core"])
                source, target = last_out.at[j, c], last_in.at[at["z"]]

                @pl.when(jnp.logical_not(here))
                def _():
                    remote(source, target, p_send.at[i, 5], p_recv.at[i, 5], device(dict(at, z=z, core=c)))

                @pl.when(here)
                def _():
                    pltpu.make_async_copy(source, target, p_recv.at[i, 5]).start()

    def stage3(i, scale):
        last_in = bufs[i][10]
        wait_all(last_in, p_recv.at[i, 5])
        total = last_in[0].astype(F32)
        for k in range(1, 8):
            total = total + last_in[k].astype(F32)
        total = total * scale
        for j, l in enumerate(CHUNKS[i]):
            parts_ref[l] = total[j]

    gp[576:608] = jnp.zeros((32, 2 * C), F32)
    joins = []
    for l in reversed(range(LAYERS)):
        d = 2**l
        rows = BACK_ROWS[l]
        half_rows = 304 if rows > 560 else 272
        for r0, r1 in ((0, half_rows), (half_rows, rows)):
            gproj[r0:r1, 0:C] = gs[r0:r1].astype(BF16)
            grad_gated = contract_columns(gproj[r0:r1], outw[l])
            filtered, opening = filt_s[l, r0:r1], open_s[l, r0:r1]
            through = grad_gated * opening
            gp[r0:r1, 0:C] = through * (1.0 - filtered * filtered)
            gp[r0:r1, C:2 * C] = through * filtered * (1.0 - opening)
        ready, joins = joins, []
        update = BACK_ROWS[l - 1] if l else T
        gpb[0:rows] = gp[0:rows].astype(BF16)
        later_b[0:update] = gp[d:d + update].astype(BF16)
        i = [l in chunk for chunk in CHUNKS].index(True)
        grads, j = bufs[i][0], CHUNKS[i].index(l)
        products = (
            contract_rows(pres_s[l], gpb[0:T]),
            contract_rows(pres_s[l], later_b[0:T]),
            contract_rows(gated_s[l], gproj[0:T]),
        )
        for half in range(2):
            for y in range(4):
                for k in range(2):
                    tile = products[k][:, y * 128:(y + 1) * 128].astype(BF16).reshape(2, 2, 4, 16, 128)
                    grads[half, y, 2 * k:2 * k + 2, j, 0:4] = tile[:, half]
                tile = products[2][:, y * 128:(y + 1) * 128].astype(BF16).reshape(4, 2, 2, 16, 128)
                grads[half, y, :, j, 4:6] = tile[:, half]
        if l == CHUNKS[i][-1]:
            remote(
                grads.at[1 - at["core"]], bufs[i][1], p_send.at[i, 0], p_recv.at[i, 0], device(peer(at, "core", 1))
            )
            waits.append((bufs[i][1], p_send.at[i, 0]))
            joins.append(i)
        for r0, r1 in ((0, 256), (256, update)):
            taps = contract_columns(gpb[r0:r1], conv[l, 0:C]) + contract_columns(
                later_b[r0:r1], conv[l, C:2 * C]
            )
            gs[r0:r1] = taps + gs[r0:r1]
        for i in ready:
            chunk_join(i)
        for i, stage in INSIDE.get(l, ()):
            (stage0, stage1)[stage](i)
        if l in (4, 2):
            hear(3 - l // 2)
            tell(4 - l // 2)
        if l == 1:
            weight_sum()
            weight_send(1, "y", 1)
    for i in joins:
        chunk_join(i)
    scale = None
    hear(3)
    for item in TAIL:
        if item == "scale":
            weight_sum()
            scale = (64.0 * 4.0 * T) / jnp.sum(wtile[4][0:1], axis=1, keepdims=True)
            gs[0:T] = gs[0:T] * scale
            out_copy = pltpu.make_async_copy(gs.at[pl.ds(0, T)], gin_hbm.at[0], out_sem)
            out_copy.start()
        elif item == "x":
            weight_sum()
            weight_send(2, "x", 4)
        elif item == "z":
            weight_sum()
            weight_send(3, "z", 7)
        elif item[1] == 0:
            stage0(item[0])
        elif item[1] == 1:
            stage1(item[0])
        elif item[1] == 2:
            stage2(item[0])
        else:
            stage3(item[0], scale)
    out_copy.wait()
    for landing, semaphore in waits:
        wait_all(landing, semaphore)
    for i in range(len(CHUNKS)):
        last_in = bufs[i][10]

        @pl.when(mine)
        def _():
            wait_all(last_in.at[pl.ds(0, 7)], p_send.at[i, 5])

        @pl.when(jnp.logical_not(mine))
        def _():
            wait_all(last_in, p_send.at[i, 5])

    for copy in halo:
        copy.wait_send()
    for group, _, _ in wcopies:
        for copy in group:
            copy.wait_send()


def deliver(gin_ref, parts_ref, gin_out, gconv_out, gout_out):
    gin_out[...] = gin_ref[...]
    core = lax.axis_index("tm") % 2
    gconv_out[...] = parts_ref[:, 0:8]
    gout_out[...] = jnp.where(core == 0, parts_ref[:, 8:12], parts_ref[:, 12:16])


def body(inputs, grad_stream_out, grad_skip_out, sample_weight, conv_weight, out_weight):
    any_spec = pl.BlockSpec(memory_space=pl.ANY)
    vmem_spec = pl.BlockSpec(memory_space=pltpu.VMEM)
    buffers = []
    for chunk in CHUNKS:
        n = len(chunk)
        shapes = (
            (2, 4, 4, n, 6), (4, 4, n, 6), (4, 4, n, 6), (3, 4, n, 3), (3, 4, n, 3), (4, n, 3), (4, n, 3),
            (3, n, 3), (3, n, 3), (4, 2, n), (8, n), (2, 2, 2, n, 3), (2, 2, 2, n, 3),
            (2, 2, n, 3), (2, 2, n, 3), (2, 2, n, 3), (2, 2, n, 3),
        )
        buffers += [pltpu.VMEM(shape + (16, 128), BF16) for shape in shapes]
    gin, parts = pl.pallas_call(
        kernel,
        name="cycle",
        out_shape=(
            jax.ShapeDtypeStruct((1, T, C), F32),
            jax.ShapeDtypeStruct((LAYERS, 16, 128), F32),
        ),
        in_specs=[any_spec] * 6,
        out_specs=(any_spec, vmem_spec),
        scratch_shapes=[
            pltpu.VMEM((EXT, C), BF16),
            pltpu.VMEM((POST, C), BF16),
            pltpu.VMEM((POST, C), BF16),
            pltpu.VMEM((1, T + 128), F32),
            pltpu.VMEM((LAYERS, 2 * C, 2 * C), BF16),
            pltpu.VMEM((LAYERS, C, 2 * C), BF16),
            pltpu.VMEM((32 + HALO + T, C), F32),
            pltpu.VMEM((LAYERS, 32, C), F32),
            pltpu.VMEM((96, C), F32),
            pltpu.VMEM((LAYERS, T, C), BF16),
            pltpu.VMEM((LAYERS, T, C), BF16),
            pltpu.VMEM((LAYERS, POST, C), F32),
            pltpu.VMEM((LAYERS, POST, C), F32),
            pltpu.VMEM((POST, C), F32),
            pltpu.VMEM((POST, 2 * C), BF16),
            pltpu.VMEM((POST + 32, 2 * C), F32),
            pltpu.VMEM((POST, 2 * C), BF16),
            pltpu.VMEM((POST, 2 * C), BF16),
            pltpu.VMEM((5, 8, 128), F32),
            pltpu.VMEM((14, 8, 128), F32),
            pltpu.SemaphoreType.DMA((16,)),
            pltpu.SemaphoreType.DMA((5,)),
            pltpu.SemaphoreType.DMA((5,)),
            pltpu.SemaphoreType.DMA((14,)),
            pltpu.SemaphoreType.DMA((14,)),
            pltpu.SemaphoreType.DMA((len(CHUNKS), 8)),
            pltpu.SemaphoreType.DMA((len(CHUNKS), 8)),
            pltpu.SemaphoreType.DMA,
            pltpu.SemaphoreType.REGULAR((4,)),
            *buffers,
        ],
        compiler_params=pltpu.CompilerParams(
            collective_id=0, has_side_effects=True, vmem_limit_bytes=58 << 20
        ),
        cost_estimate=pl.CostEstimate(flops=8 * 10**9, bytes_accessed=8 * 10**6, transcendentals=4 * 10**6),
    )(inputs, grad_stream_out, grad_skip_out, sample_weight, conv_weight, out_weight)
    return pl.pallas_call(
        deliver,
        name="deliver",
        out_shape=(
            jax.ShapeDtypeStruct((1, T, C), F32),
            jax.ShapeDtypeStruct((LAYERS, 8, 128), F32),
            jax.ShapeDtypeStruct((LAYERS, 4, 128), F32),
        ),
        in_specs=[vmem_spec, vmem_spec],
        out_specs=(vmem_spec, vmem_spec, vmem_spec),
    )(gin, parts)


def solution(mesh):
    placed = (
        P("dp", "tm", None),
        P("dp", "tm", None),
        P("dp", "tm", None),
        P("dp", "tm"),
        P(),
        P(),
    )
    return jax.shard_map(
        body,
        mesh=mesh,
        in_specs=placed,
        out_specs=(P("dp", "tm", None), P(None, "tm", "dp"), P(None, "tm", "dp")),
        check_vma=False,
    )
```

```python
import functools

import jax
import jax.numpy as jnp
from jax import lax
from jax.experimental import pallas as pl
from jax.experimental.pallas import tpu as pltpu
from jax.sharding import PartitionSpec as P

MESH = pl.DeviceIdType.MESH
F32, BF16 = jnp.float32, jnp.bfloat16
C, LAYERS, T, HALO = 256, 6, 512, 64
EXT = T + 2 * HALO
POST = T + HALO
SIZES = {"x": 4, "y": 4, "z": 8}
BACK_ROWS = (544, 544, 544, 544, 544, 576)
START = (0, 0, 0, 16, 32, 64)
FIRST = (80, 96, 112, 128, 144, 176)
MIDDLE = 336
BUFFERS = 17
CHUNKS = ((5,), (4, 3), (2, 1), (0,))
HALVED = (0, 1, 2)
INSIDE = {1: ((0, 0),), 0: ((1, 0), (0, 1))}
TAIL = (
    "x", (2, 0), (1, 1), (0, 2), "z", (3, 1), (2, 1), (1, 2), (3, 2), (2, 2), "scale", (0, 3), (1, 3),
    (3, 3), (2, 3),
)


def contract_rows(left, right):
    return lax.dot_general(left, right, (((0,), (0,)), ((), ())), preferred_element_type=F32)


def contract_columns(left, right):
    return lax.dot_general(left, right, (((1,), (1,)), ((), ())), preferred_element_type=F32)


def place():
    tm, y = lax.axis_index("tm"), lax.axis_index("dp")
    return {"x": tm // 16, "y": y, "z": (tm // 2) % 8, "core": tm % 2}


def device(at):
    return ((at["x"] * 8 + at["z"]) * 2 + at["core"], at["y"])


def flips(i):
    return (i + 1 - 2 * (i % 2), 3 - i), (3 - i, i + 1 - 2 * (i % 2))


def peer(at, axis, step):
    if axis == "core":
        return dict(at, core=1 - at["core"])
    return dict(at, **{axis: (at[axis] + step) % SIZES[axis]})


def remote(src, dst, send, recv, target):
    copy = pltpu.make_async_remote_copy(
        src_ref=src, dst_ref=dst, send_sem=send, recv_sem=recv,
        device_id=target, device_id_type=MESH,
    )
    copy.start()
    return copy


def kernel(
    x_hbm, gso_hbm, gsk_hbm, sw_hbm, conv_hbm, outw_hbm,
    gin_hbm, parts_ref,
    xe, gse, gke, swe, conv, outw,
    stream, tail_s, postb, pres_s, gated_s, filt_s, open_s,
    gs, gproj, gp, gpb, later_b, wtile, wrecv,
    load_sem, halo_send, halo_recv, w_send, w_recv, p_send, p_recv, out_sem, known, *rest,
):
    bufs = [rest[BUFFERS * i:BUFFERS * (i + 1)] for i in range(len(CHUNKS))]
    at = place()
    tm = lax.axis_index("tm")
    nxt = ((tm + 1) % 64, at["y"])
    prv = ((tm + 63) % 64, at["y"])

    barrier = pltpu.get_barrier_semaphore()
    greet = [nxt, prv, device(peer(at, "core", 1))]
    for axis in "yxz":
        greet += [device(peer(at, axis, 1)), device(peer(at, axis, SIZES[axis] - 1))]
    for target in greet:
        pl.semaphore_signal(barrier, inc=1, device_id=target, device_id_type=MESH)

    loads = [
        pltpu.make_async_copy(x_hbm.at[0], xe.at[pl.ds(HALO, T)], load_sem.at[0]),
        pltpu.make_async_copy(sw_hbm, swe.at[:, pl.ds(0, T)], load_sem.at[1]),
    ]
    for l in range(LAYERS):
        loads.append(pltpu.make_async_copy(conv_hbm.at[l], conv.at[l], load_sem.at[4 + l]))
        loads.append(pltpu.make_async_copy(outw_hbm.at[l], outw.at[l], load_sem.at[10 + l]))
    loads.append(pltpu.make_async_copy(gso_hbm.at[0], gse.at[pl.ds(0, T)], load_sem.at[2]))
    loads.append(pltpu.make_async_copy(gsk_hbm.at[0], gke.at[pl.ds(0, T)], load_sem.at[3]))
    for copy in loads[:6]:
        copy.start()

    pl.semaphore_wait(barrier, len(greet))

    def tell(step):
        for k in (1, SIZES["z"] - 1):
            pl.semaphore_signal(known.at[step], inc=1, device_id=device(peer(at, "z", k)), device_id_type=MESH)

    def hear(step):
        pl.semaphore_wait(known.at[step], 2)

    tell(0)
    first, final = pl.ds(0, HALO), pl.ds(T, HALO)
    halo = [
        remote(x_hbm.at[0, pl.ds(T - HALO, HALO)], xe.at[first], halo_send.at[0], halo_recv.at[0], nxt),
        remote(x_hbm.at[0, first], xe.at[pl.ds(HALO + T, HALO)], halo_send.at[1], halo_recv.at[1], prv),
        remote(gso_hbm.at[0, first], gse.at[final], halo_send.at[2], halo_recv.at[2], prv),
        remote(gsk_hbm.at[0, first], gke.at[final], halo_send.at[3], halo_recv.at[3], prv),
        remote(sw_hbm.at[:, pl.ds(0, 128)], swe.at[:, pl.ds(T, 128)], halo_send.at[4], halo_recv.at[4], prv),
    ]

    def activate(l, present, earlier):
        preact = jnp.dot(present, conv[l, 0:C], preferred_element_type=F32) + jnp.dot(
            earlier, conv[l, C:2 * C], preferred_element_type=F32
        )
        filtered = jnp.tanh(preact[:, :C])
        opening = 0.5 * jnp.tanh(0.5 * preact[:, C:]) + 0.5
        return filtered, opening, (filtered * opening).astype(BF16)

    loads[0].wait()
    stream[32 + HALO:32 + HALO + T] = xe[HALO:HALO + T].astype(F32)
    wcopies = []
    for l in range(LAYERS):
        d = 2**l
        loads[2 + 2 * l].wait()
        loads[3 + 2 * l].wait()
        for copy in loads[6 + 2 * l:8 + 2 * l]:
            copy.start()
        tail_s[l] = stream[HALO + T:HALO + T + 32]
        for lo, hi in ((MIDDLE, HALO + T), (FIRST[l], MIDDLE)):
            present = stream[32 + lo:32 + hi].astype(BF16)
            filtered, opening, gated = activate(l, present, stream[32 + lo - d:32 + hi - d].astype(BF16))
            filt_s[l, lo - HALO:hi - HALO] = filtered
            open_s[l, lo - HALO:hi - HALO] = opening
            pres_s[l, lo - HALO:hi - HALO] = present
            gated_s[l, lo - HALO:hi - HALO] = gated
            if l < LAYERS - 1:
                stream[32 + lo:32 + hi] += jnp.dot(gated, outw[l, :, 0:C], preferred_element_type=F32)

    loads[1].wait()
    wtile[0] = jnp.broadcast_to(
        swe[:, 0:128] + swe[:, 128:256] + swe[:, 256:384] + swe[:, 384:512], (8, 128)
    )

    def weight_send(step, axis, base):
        group = []
        for k in range(1, 2 if axis == "core" else SIZES[axis]):
            slot = base + k - 1
            group.append(remote(
                wtile.at[step], wrecv.at[slot], w_send.at[slot], w_recv.at[slot], device(peer(at, axis, k))
            ))
        wcopies.append((group, step, base))

    def weight_sum():
        group, step, base = wcopies[-1]
        total = wtile[step]
        for k, copy in enumerate(group):
            copy.wait_recv()
            total = total + wrecv[base + k]
        wtile[step + 1] = total

    weight_send(0, "core", 0)

    loads[-2].wait()
    loads[-1].wait()

    def weigh(b, rows):
        lo = 128 * b
        weighting = jnp.broadcast_to(swe[:, lo:lo + 128], (128, 128)).T[:rows]
        if lo == T:
            weighting = jnp.where(tm == 63, 0.0, weighting)
        weighting = jnp.concatenate([weighting, weighting], axis=1)
        gs[lo:lo + rows] = gse[lo:lo + rows].astype(F32) * weighting
        gproj[lo:lo + rows, C:2 * C] = (gke[lo:lo + rows].astype(F32) * weighting).astype(BF16)

    for b in range(4):
        weigh(b, 128)

    stream[0:32] = jnp.zeros((32, C), F32)
    halo[0].wait_recv()
    halo[1].wait_recv()
    stream[32:32 + HALO] = jnp.where(tm == 0, 0.0, xe[0:HALO].astype(F32))
    postb[32:96] = xe[HALO + T:].astype(F32)
    for l in range(LAYERS):
        d = 2**l
        lo, hi = START[l], FIRST[l]
        count = hi - lo
        postb[0:32] = tail_s[l]
        present = jnp.concatenate([stream[32 + lo:32 + hi], postb[32:96]], axis=0).astype(BF16)
        earlier = jnp.concatenate([stream[32 + lo - d:32 + hi - d], postb[32 - d:96 - d]], axis=0).astype(BF16)
        filtered, opening, gated = activate(l, present, earlier)
        skip = HALO - lo
        filt_s[l, 0:hi - HALO] = filtered[skip:count]
        open_s[l, 0:hi - HALO] = opening[skip:count]
        pres_s[l, 0:hi - HALO] = present[skip:count]
        gated_s[l, 0:hi - HALO] = gated[skip:count]
        filt_s[l, T:POST] = filtered[count:]
        open_s[l, T:POST] = opening[count:]
        if l < LAYERS - 1:
            projected = jnp.dot(gated, outw[l, :, 0:C], preferred_element_type=F32)
            stream[32 + lo:32 + hi] += projected[:count]
            postb[32:96] += projected[count:]
    for i in (2, 3, 4):
        halo[i].wait_recv()
    hear(0)
    tell(1)
    weigh(4, HALO)

    waits = []

    def send_all(axis, pick_source, landing, send, recv):
        for k in range(1, SIZES[axis]):
            other = peer(at, axis, k)
            remote(pick_source(other[axis]), landing.at[k - 1], send, recv, device(other))
        waits.append((landing, send))

    def wait_all(landing, semaphore):
        pltpu.make_async_copy(landing, landing, semaphore).wait()

    def collect(own, landing):
        low = own.astype(F32) + landing[0].astype(F32)
        return low + (landing[1].astype(F32) + landing[2].astype(F32))

    def chunk_join(i):
        grads, other, held, y_in, x_in = bufs[i][:5]
        wait_all(other, p_recv.at[i, 0])
        held[...] = grads[at["core"]] + other[...]
        if i in HALVED:
            for k, axis in enumerate("yx"):
                for half, (target, _) in enumerate(flips(at[axis])):
                    for slot, block in enumerate((target, (at[axis] + 2) % 4)):
                        remote(
                            held.at[quarter(axis, block, half)], bufs[i][11 + k].at[half, slot],
                            p_send.at[i, 1 + k], p_recv.at[i, 1 + k], device(dict(at, **{axis: target})),
                        )
                waits.append((bufs[i][11 + k], p_send.at[i, 1 + k]))
            return
        send_all("y", lambda y: held.at[y, :, :, pl.ds(0, 3)], y_in, p_send.at[i, 1], p_recv.at[i, 1])
        send_all("x", lambda x: held.at[:, x, :, pl.ds(3, 3)], x_in, p_send.at[i, 2], p_recv.at[i, 2])

    def quarter(axis, block, half):
        rest = pl.ds(2 * half, 2)
        if axis == "y":
            return block, rest, slice(None), pl.ds(0, 3)
        return rest, block, slice(None), pl.ds(3, 3)

    def stage0(i):
        held = bufs[i][2]
        for k, axis in enumerate("yx"):
            arrived, kept, final_in = bufs[i][11 + k], bufs[i][13 + k], bufs[i][15 + k]
            wait_all(arrived, p_recv.at[i, 1 + k])
            for half, (_, target) in enumerate(flips(at[axis])):
                kept[half] = held[quarter(axis, target, half)] + arrived[half, 1]
                remote(
                    kept.at[half], final_in.at[half], p_send.at[i, 6 + k], p_recv.at[i, 6 + k],
                    device(dict(at, **{axis: target})),
                )
            waits.append((final_in, p_send.at[i, 6 + k]))

    def halved_sum(i, k):
        axis = "yx"[k]
        held, arrived, final_in, total = bufs[i][2], bufs[i][11 + k], bufs[i][15 + k], bufs[i][5 + k]
        wait_all(final_in, p_recv.at[i, 6 + k])
        for half in range(2):
            own = held[quarter(axis, at[axis], half)].astype(F32) + arrived[half, 0].astype(F32)
            total[2 * half:2 * half + 2] = (own + final_in[half].astype(F32)).astype(BF16)

    def stage1(i):
        held, y_in, x_in, y_sum, x_sum, yx_in, xy_in = bufs[i][2:9]
        if i in HALVED:
            halved_sum(i, 0)
        else:
            wait_all(y_in, p_recv.at[i, 1])
            y_sum[...] = collect(held[at["y"], :, :, 0:3], y_in).astype(BF16)
        send_all("x", lambda x: y_sum.at[x], yx_in, p_send.at[i, 3], p_recv.at[i, 3])
        if i in HALVED:
            halved_sum(i, 1)
        else:
            wait_all(x_in, p_recv.at[i, 2])
            x_sum[...] = collect(held[:, at["x"], :, 3:6], x_in).astype(BF16)
        send_all("y", lambda y: x_sum.at[y], xy_in, p_send.at[i, 4], p_recv.at[i, 4])

    mine = at["z"] // 4 == at["core"]

    def stage2(i):
        y_sum, x_sum, yx_in, xy_in, last_out, last_in = bufs[i][5:11]
        wait_all(yx_in, p_recv.at[i, 3])
        tiles = [collect(y_sum[at["x"]], yx_in)]
        wait_all(xy_in, p_recv.at[i, 4])
        tiles.append(collect(x_sum[at["y"]], xy_in))
        for j in range(4):
            rows = tiles[j // 3][:, j % 3]
            out_rows = tiles[1][:, 1 + j // 2, 8 * (j % 2):8 * (j % 2) + 8]
            for c in range(2):
                last_out[j, c] = jnp.concatenate([rows[:, 8 * c:8 * c + 8], out_rows], axis=1).astype(BF16)
        for j in range(4):
            for c in range(2):
                z = 4 * at["core"] + j
                here = jnp.logical_and(z == at["z"], c == at["core"])
                source, target = last_out.at[j, c], last_in.at[at["z"]]

                @pl.when(jnp.logical_not(here))
                def _():
                    remote(source, target, p_send.at[i, 5], p_recv.at[i, 5], device(dict(at, z=z, core=c)))

                @pl.when(here)
                def _():
                    pltpu.make_async_copy(source, target, p_recv.at[i, 5]).start()

    def stage3(i, scale):
        last_in = bufs[i][10]
        wait_all(last_in, p_recv.at[i, 5])
        total = last_in[0].astype(F32)
        for k in range(1, 8):
            total = total + last_in[k].astype(F32)
        total = total * scale
        for j, l in enumerate(CHUNKS[i]):
            parts_ref[l] = total[j]

    gp[576:608] = jnp.zeros((32, 2 * C), F32)
    def tap_products(l, update):
        for r0, r1 in ((0, 256), (256, update)):
            taps = contract_columns(gpb[r0:r1], conv[l, 0:C]) + contract_columns(
                later_b[r0:r1], conv[l, C:2 * C]
            )
            gs[r0:r1] = taps + gs[r0:r1]

    joins = []
    for l in reversed(range(LAYERS)):
        d = 2**l
        rows = BACK_ROWS[l]
        half_rows = 304 if rows > 560 else 272
        for r0, r1 in ((0, half_rows), (half_rows, rows)):
            gproj[r0:r1, 0:C] = gs[r0:r1].astype(BF16)
            grad_gated = contract_columns(gproj[r0:r1], outw[l])
            filtered, opening = filt_s[l, r0:r1], open_s[l, r0:r1]
            through = grad_gated * opening
            gp[r0:r1, 0:C] = through * (1.0 - filtered * filtered)
            gp[r0:r1, C:2 * C] = through * filtered * (1.0 - opening)
        ready, joins = joins, []
        update = BACK_ROWS[l - 1] if l else T
        gpb[0:rows] = gp[0:rows].astype(BF16)
        later_b[0:update] = gp[d:d + update].astype(BF16)
        i = [l in chunk for chunk in CHUNKS].index(True)
        grads, j = bufs[i][0], CHUNKS[i].index(l)
        products = (
            contract_rows(pres_s[l], gpb[0:T]),
            contract_rows(pres_s[l], later_b[0:T]),
            contract_rows(gated_s[l], gproj[0:T]),
        )
        for half in range(2):
            for y in range(4):
                for k in range(2):
                    tile = products[k][:, y * 128:(y + 1) * 128].astype(BF16).reshape(2, 2, 4, 16, 128)
                    grads[half, y, 2 * k:2 * k + 2, j, 0:4] = tile[:, half]
                tile = products[2][:, y * 128:(y + 1) * 128].astype(BF16).reshape(4, 2, 2, 16, 128)
                grads[half, y, :, j, 4:6] = tile[:, half]
        if l == CHUNKS[i][-1]:
            remote(
                grads.at[1 - at["core"]], bufs[i][1], p_send.at[i, 0], p_recv.at[i, 0], device(peer(at, "core", 1))
            )
            waits.append((bufs[i][1], p_send.at[i, 0]))
            joins.append(i)
        if l:
            tap_products(l, update)
        for i in ready:
            chunk_join(i)
        for i, stage in INSIDE.get(l, ()):
            (stage0, stage1)[stage](i)
        if l in (4, 2):
            hear(3 - l // 2)
            tell(4 - l // 2)
        if l == 1:
            weight_sum()
            weight_send(1, "y", 1)
    for i in joins:
        chunk_join(i)
    tap_products(0, T)
    scale = None
    hear(3)
    for item in TAIL:
        if item == "scale":
            weight_sum()
            scale = (64.0 * 4.0 * T) / jnp.sum(wtile[4][0:1], axis=1, keepdims=True)
            gs[0:T] = gs[0:T] * scale
            out_copy = pltpu.make_async_copy(gs.at[pl.ds(0, T)], gin_hbm.at[0], out_sem)
            out_copy.start()
        elif item == "x":
            weight_sum()
            weight_send(2, "x", 4)
        elif item == "z":
            weight_sum()
            weight_send(3, "z", 7)
        elif item[1] == 0:
            stage0(item[0])
        elif item[1] == 1:
            stage1(item[0])
        elif item[1] == 2:
            stage2(item[0])
        else:
            stage3(item[0], scale)
    out_copy.wait()
    for landing, semaphore in waits:
        wait_all(landing, semaphore)
    for i in range(len(CHUNKS)):
        last_in = bufs[i][10]

        @pl.when(mine)
        def _():
            wait_all(last_in.at[pl.ds(0, 7)], p_send.at[i, 5])

        @pl.when(jnp.logical_not(mine))
        def _():
            wait_all(last_in, p_send.at[i, 5])

    for copy in halo:
        copy.wait_send()
    for group, _, _ in wcopies:
        for copy in group:
            copy.wait_send()


def deliver(gin_ref, parts_ref, gin_out, gconv_out, gout_out):
    gin_out[...] = gin_ref[...]
    core = lax.axis_index("tm") % 2
    gconv_out[...] = parts_ref[:, 0:8]
    gout_out[...] = jnp.where(core == 0, parts_ref[:, 8:12], parts_ref[:, 12:16])


def body(inputs, grad_stream_out, grad_skip_out, sample_weight, conv_weight, out_weight):
    any_spec = pl.BlockSpec(memory_space=pl.ANY)
    vmem_spec = pl.BlockSpec(memory_space=pltpu.VMEM)
    buffers = []
    for chunk in CHUNKS:
        n = len(chunk)
        shapes = (
            (2, 4, 4, n, 6), (4, 4, n, 6), (4, 4, n, 6), (3, 4, n, 3), (3, 4, n, 3), (4, n, 3), (4, n, 3),
            (3, n, 3), (3, n, 3), (4, 2, n), (8, n), (2, 2, 2, n, 3), (2, 2, 2, n, 3),
            (2, 2, n, 3), (2, 2, n, 3), (2, 2, n, 3), (2, 2, n, 3),
        )
        buffers += [pltpu.VMEM(shape + (16, 128), BF16) for shape in shapes]
    gin, parts = pl.pallas_call(
        kernel,
        name="cycle",
        out_shape=(
            jax.ShapeDtypeStruct((1, T, C), F32),
            jax.ShapeDtypeStruct((LAYERS, 16, 128), F32),
        ),
        in_specs=[any_spec] * 6,
        out_specs=(any_spec, vmem_spec),
        scratch_shapes=[
            pltpu.VMEM((EXT, C), BF16),
            pltpu.VMEM((POST, C), BF16),
            pltpu.VMEM((POST, C), BF16),
            pltpu.VMEM((1, T + 128), F32),
            pltpu.VMEM((LAYERS, 2 * C, 2 * C), BF16),
            pltpu.VMEM((LAYERS, C, 2 * C), BF16),
            pltpu.VMEM((32 + HALO + T, C), F32),
            pltpu.VMEM((LAYERS, 32, C), F32),
            pltpu.VMEM((96, C), F32),
            pltpu.VMEM((LAYERS, T, C), BF16),
            pltpu.VMEM((LAYERS, T, C), BF16),
            pltpu.VMEM((LAYERS, POST, C), F32),
            pltpu.VMEM((LAYERS, POST, C), F32),
            pltpu.VMEM((POST, C), F32),
            pltpu.VMEM((POST, 2 * C), BF16),
            pltpu.VMEM((POST + 32, 2 * C), F32),
            pltpu.VMEM((POST, 2 * C), BF16),
            pltpu.VMEM((POST, 2 * C), BF16),
            pltpu.VMEM((5, 8, 128), F32),
            pltpu.VMEM((14, 8, 128), F32),
            pltpu.SemaphoreType.DMA((16,)),
            pltpu.SemaphoreType.DMA((5,)),
            pltpu.SemaphoreType.DMA((5,)),
            pltpu.SemaphoreType.DMA((14,)),
            pltpu.SemaphoreType.DMA((14,)),
            pltpu.SemaphoreType.DMA((len(CHUNKS), 8)),
            pltpu.SemaphoreType.DMA((len(CHUNKS), 8)),
            pltpu.SemaphoreType.DMA,
            pltpu.SemaphoreType.REGULAR((4,)),
            *buffers,
        ],
        compiler_params=pltpu.CompilerParams(
            collective_id=0, has_side_effects=True, vmem_limit_bytes=58 << 20
        ),
        cost_estimate=pl.CostEstimate(flops=8 * 10**9, bytes_accessed=8 * 10**6, transcendentals=4 * 10**6),
    )(inputs, grad_stream_out, grad_skip_out, sample_weight, conv_weight, out_weight)
    return pl.pallas_call(
        deliver,
        name="deliver",
        out_shape=(
            jax.ShapeDtypeStruct((1, T, C), F32),
            jax.ShapeDtypeStruct((LAYERS, 8, 128), F32),
            jax.ShapeDtypeStruct((LAYERS, 4, 128), F32),
        ),
        in_specs=[vmem_spec, vmem_spec],
        out_specs=(vmem_spec, vmem_spec, vmem_spec),
    )(gin, parts)


def solution(mesh):
    placed = (
        P("dp", "tm", None),
        P("dp", "tm", None),
        P("dp", "tm", None),
        P("dp", "tm"),
        P(),
        P(),
    )
    return jax.shard_map(
        body,
        mesh=mesh,
        in_specs=placed,
        out_specs=(P("dp", "tm", None), P(None, "tm", "dp"), P(None, "tm", "dp")),
        check_vma=False,
    )
```
